1024 devices in a mesh: pp: 16 (over y_lo, x, core), ep: 64 (over y_hi, z).
Axes of the slice: x: 4, y: 8 (y_hi: 4, y_lo: 2; y = y_hi * 2 + y_lo), z: 16, core: 2. Of those that a mesh axis runs over, the one named last changes fastest.
Arguments:
- x_fwd: bfloat16 [16, 4096, 7168], P('pp', 'ep'), may hold values from -6 to 6
- dy_bwd: bfloat16 [16, 4096, 7168], P('pp', 'ep'), may hold values from -6 to 6
- routes_fwd: int32 [16, 4096, 8], P('pp', 'ep'), may hold values from 0 to 255, as said below
- routes_bwd: int32 [16, 4096, 8], P('pp', 'ep'), may hold values from 0 to 255, as said below
- score_fwd: float32 [16, 4096, 8], P('pp', 'ep'), may hold values from 0.05 to 1
- score_bwd: float32 [16, 4096, 8], P('pp', 'ep'), may hold values from 0.05 to 1
- saved_bwd: float32 [16, 64, 2, 2, 8192], P('pp', None, None, None, 'ep'), may hold values from -6 to 6
- w_gate: bfloat16 [7168, 8192], P(None, 'ep'), may hold values from -0.0625 to 0.0625
- w_up: bfloat16 [7168, 8192], P(None, 'ep'), may hold values from -0.0625 to 0.0625
- w_down: bfloat16 [8192, 7168], P('ep'), may hold values from -0.1875 to 0.1875
Outputs:
- received: bfloat16 [16, 4096, 7168], P('pp', 'ep')
The draws below stay inside these ranges and needn't reach their ends.
Inputs may be any that keep to these rules, and one draw needn't show every extreme that they name: `routes_fwd`: each token names 8 different ids. Within the 64 tokens of one block of a section, each expert below 8 is named at most 2 times, and in every section some expert below 8 is named exactly 2 times in every block. `routes_bwd`: the same as for routes_fwd.
All inputs are finite; a program needn't handle non-finite values.
Results may differ from the reference program's by a relative error of at most 0.008.
Values may be sent and summed in bfloat16 or wider, within the bound.
No kernel may reach another device: no remote copies, remote signals or barrier semaphores. Data moves between devices by JAX's collectives and lax.ppermute only.
A program may use at most 64 MiB of HBM per device.

```python
import math
import jax
import jax.numpy as jnp
from jax import lax

D = 7168
EXPERTS = 256
TOPK = 8
HID_DEV = 128
SPLIT = 8
CAP = 2
TOK_DEV = 64
HID = 1024
EXP_SECTION = 8
SECTIONS = 16
TOKENS = 4096
N_EP = 64


def route_draw(key, salt):
    key = jax.random.fold_in(key, salt)
    keys = jax.random.split(key, 5)
    blocks = TOKENS // TOK_DEV
    total_tokens = SECTIONS * TOKENS
    hot_expert = jax.random.randint(keys[0], (SECTIONS, 1, 1), 0, EXP_SECTION)
    counts = jax.random.randint(keys[1], (SECTIONS, blocks, EXP_SECTION), 0, CAP + 1)
    expert_ids = jnp.arange(EXP_SECTION, dtype=jnp.int32)[None, None, :]
    counts = jnp.where(expert_ids == hot_expert, CAP, counts)
    token_scores = jax.random.randint(keys[2], (SECTIONS, blocks, EXP_SECTION, TOK_DEV), 0, 1 << 20) * TOK_DEV
    token_scores = token_scores + jnp.arange(TOK_DEV, dtype=jnp.int32)
    ranks = jnp.argsort(jnp.argsort(token_scores, axis=-1), axis=-1)
    flagged = (ranks < counts[..., None]).astype(jnp.int32)
    flagged = jnp.transpose(flagged, (0, 1, 3, 2)).reshape(total_tokens, EXP_SECTION)
    order_keys = (1 - flagged) * EXP_SECTION + jnp.arange(EXP_SECTION, dtype=jnp.int32)[None, :]
    window_ids = jnp.argsort(order_keys, axis=-1).astype(jnp.int32)
    window_count = jnp.sum(flagged, axis=-1)
    if TOPK > EXP_SECTION:
        window_ids = jnp.concatenate([window_ids, jnp.zeros((total_tokens, TOPK - EXP_SECTION), jnp.int32)], axis=1)
    perm_keys = jax.random.split(keys[3], total_tokens)
    others = jax.vmap(lambda one_key: jax.random.permutation(one_key, EXPERTS - EXP_SECTION)[:TOPK])(perm_keys)
    others = others.astype(jnp.int32) + EXP_SECTION
    positions = jnp.arange(TOPK, dtype=jnp.int32)[None, :]
    chosen = jnp.where(positions < window_count[:, None], window_ids[:, :TOPK], others)
    shuffle_scores = jax.random.randint(keys[4], (total_tokens, TOPK), 0, 1 << 20) * TOPK + positions
    shuffle_order = jnp.argsort(shuffle_scores, axis=-1)
    chosen = jnp.take_along_axis(chosen, shuffle_order, axis=-1)
    return chosen.reshape(SECTIONS, TOKENS, TOPK).astype(jnp.int32)


def draw_routes_fwd(key, part):
    return route_draw(key, 101)


def draw_routes_bwd(key, part):
    return route_draw(key, 202)


def levels(stream_key, dims, shards, low, largest):
    level = 1.0
    for axis_at, shards_of in shards:
        steps = jax.random.uniform(jax.random.fold_in(jax.random.fold_in(stream_key, 6), axis_at), (shards_of,), jnp.float32, low / len(shards), largest / len(shards))
        level = level * jnp.repeat(jnp.exp(steps), dims[axis_at] // shards_of).reshape((-1,) + (1,) * (len(dims) - 1 - axis_at))
    return level


def gaussian(own_key, extent, width, bound, cuts=(), kind=jnp.bfloat16):
    gain = levels(own_key, extent, cuts, -0.22, 0.18) if cuts else 1.0
    result = jax.random.normal(own_key, extent, jnp.float32) * width * gain
    return jnp.minimum(jnp.maximum(result, -bound), bound).astype(kind)


def setup_inputs(seed: int = 0) -> dict:
    streams_of = jax.random.split(jax.random.key(seed), 11)
    return {
        "x_fwd": gaussian(streams_of[0], (SECTIONS, TOKENS, D), 1.0, 6.0, ((0, 16), (1, 64))),
        "dy_bwd": gaussian(streams_of[1], (SECTIONS, TOKENS, D), 1.0, 6.0, ((0, 16), (1, 64))),
        "routes_fwd": draw_routes_fwd(jax.random.fold_in(streams_of[10], 71), 0),
        "routes_bwd": draw_routes_bwd(jax.random.fold_in(streams_of[10], 71), 0),
        "score_fwd": jnp.clip(jnp.exp(math.log(1.0) - 2.9957323 * jax.random.uniform(streams_of[4], (SECTIONS, TOKENS, TOPK), jnp.float32) ** levels(streams_of[4], (SECTIONS, TOKENS, TOPK), ((0, 16), (1, 64)), -0.2, 0.2)), 0.05, 1.0),
        "score_bwd": jnp.clip(jnp.exp(math.log(1.0) - 2.9957323 * jax.random.uniform(streams_of[5], (SECTIONS, TOKENS, TOPK), jnp.float32) ** levels(streams_of[5], (SECTIONS, TOKENS, TOPK), ((0, 16), (1, 64)), -0.2, 0.2)), 0.05, 1.0),
        "saved_bwd": gaussian(streams_of[6], (SECTIONS, N_EP, CAP, 2, EXP_SECTION * HID), 1.0, 6.0, ((0, 16), (4, 64)), jnp.float32),
        "w_gate": gaussian(streams_of[7], (D, EXP_SECTION * HID), D ** -0.5, 0.0625, ((1, 64),)),
        "w_up": gaussian(streams_of[8], (D, EXP_SECTION * HID), D ** -0.5, 0.0625, ((1, 64),)),
        "w_down": gaussian(streams_of[9], (EXP_SECTION * HID, D), HID ** -0.5, 0.1875, ((0, 64),)),
    }


def route_tables(routes, scores):
    experts = jnp.arange(EXP_SECTION, dtype=jnp.int32)
    match = (routes[..., None] == experts).astype(jnp.float32)
    weight = 2.5 * scores / jnp.sum(scores, axis=-1, keepdims=True)
    hits = jnp.sum(match, axis=2)
    shares = jnp.sum(match * weight[..., None], axis=2)
    before = jnp.cumsum(hits, axis=1) - hits
    slots = jnp.arange(CAP, dtype=jnp.float32)
    placed = hits[..., None] * (before[..., None] == slots).astype(jnp.float32)
    return placed, placed * shares[..., None]


def gather_slots(placed, values):
    return jnp.einsum('btgc,btd->gbcd', placed, values.astype(jnp.float32)).astype(jnp.bfloat16)


def combine_slots(weighted, expert_out):
    return jnp.einsum('btgc,gbcd->btd', weighted, expert_out, precision=lax.Precision.HIGHEST)


def reference(x_fwd, dy_bwd, routes_fwd, routes_bwd, score_fwd, score_bwd, saved_bwd, w_gate, w_up, w_down):
    contract = (((1,), (1,)), ((), ()))

    def forward_expert(inputs):
        token_rows, expert = inputs
        flat_rows = token_rows.reshape(-1, D)
        first_col = (expert * HID).astype(jnp.int32)
        gate_cols = lax.dynamic_slice_in_dim(w_gate, first_col, HID, 1)
        up_cols = lax.dynamic_slice_in_dim(w_up, first_col, HID, 1)
        down_rows = lax.dynamic_slice_in_dim(w_down, first_col, HID, 0)
        gate_pre = jnp.dot(flat_rows, gate_cols, preferred_element_type=jnp.float32)
        up_pre = jnp.dot(flat_rows, up_cols, preferred_element_type=jnp.float32)
        hidden = (jax.nn.silu(gate_pre) * up_pre).astype(jnp.bfloat16)
        summed = jnp.zeros((flat_rows.shape[0], D), jnp.float32)
        for split_index in range(SPLIT):
            lower = split_index * HID_DEV
            partial_value = jnp.dot(hidden[:, lower:lower + HID_DEV], down_rows[lower:lower + HID_DEV],
                              preferred_element_type=jnp.float32)
            rounded = lax.optimization_barrier(partial_value.astype(jnp.bfloat16))
            summed = summed + rounded.astype(jnp.float32)
        return summed.reshape(token_rows.shape[0], token_rows.shape[1], D)

    def one_section(inputs):
        x_section, dy_section, routes_a, routes_b, score_a, score_b, saved_section = inputs
        experts = jnp.arange(EXP_SECTION, dtype=jnp.int32)

        def backward_expert(inner):
            token_rows, expert = inner
            flat_rows = token_rows.reshape(-1, D)
            first_col = (expert * HID).astype(jnp.int32)
            gate_cols = lax.dynamic_slice_in_dim(w_gate, first_col, HID, 1)
            up_cols = lax.dynamic_slice_in_dim(w_up, first_col, HID, 1)
            down_rows = lax.dynamic_slice_in_dim(w_down, first_col, HID, 0)
            gate_saved = lax.dynamic_slice_in_dim(saved_section[:, :, 0], first_col, HID, 2).reshape(-1, HID)
            up_saved = lax.dynamic_slice_in_dim(saved_section[:, :, 1], first_col, HID, 2).reshape(-1, HID)
            grad_hidden = lax.dot_general(flat_rows, down_rows, contract, preferred_element_type=jnp.float32)
            sigma = jax.nn.sigmoid(gate_saved)
            grad_gate = (grad_hidden * up_saved * sigma * (1.0 + gate_saved * (1.0 - sigma))).astype(jnp.bfloat16)
            grad_up = (grad_hidden * gate_saved * sigma).astype(jnp.bfloat16)
            summed = jnp.zeros((flat_rows.shape[0], D), jnp.float32)
            for split_index in range(SPLIT):
                lower = split_index * HID_DEV
                upper = lower + HID_DEV
                partial_value = lax.dot_general(grad_gate[:, lower:upper], gate_cols[:, lower:upper], contract,
                                          preferred_element_type=jnp.float32)
                partial_value = partial_value + lax.dot_general(grad_up[:, lower:upper], up_cols[:, lower:upper], contract,
                                                    preferred_element_type=jnp.float32)
                rounded = lax.optimization_barrier(partial_value.astype(jnp.bfloat16))
                summed = summed + rounded.astype(jnp.float32)
            return summed.reshape(token_rows.shape[0], token_rows.shape[1], D)

        placed_f, weighted_f = route_tables(routes_a.reshape(N_EP, TOK_DEV, TOPK), score_a.reshape(N_EP, TOK_DEV, TOPK))
        rows_f = gather_slots(placed_f, x_section.reshape(N_EP, TOK_DEV, D))
        out_f = lax.map(forward_expert, (rows_f, experts))
        routed_f = combine_slots(weighted_f, out_f).reshape(TOKENS, D).astype(jnp.bfloat16)
        placed_b, weighted_b = route_tables(routes_b.reshape(N_EP, TOK_DEV, TOPK), score_b.reshape(N_EP, TOK_DEV, TOPK))
        rows_b = gather_slots(placed_b, dy_section.reshape(N_EP, TOK_DEV, D))
        out_b = lax.map(backward_expert, (rows_b, experts))
        routed_b = combine_slots(weighted_b, out_b).reshape(TOKENS, D).astype(jnp.bfloat16)
        return routed_f, routed_b

    routed_f, routed_b = lax.map(one_section, (x_fwd, dy_bwd, routes_fwd, routes_bwd, score_fwd, score_bwd, saved_bwd))
    total = jnp.roll(routed_f, 1, axis=0).astype(jnp.float32) + jnp.roll(routed_b, -1, axis=0).astype(jnp.float32)
    return total.astype(jnp.bfloat16)
```

```python
import functools

import jax
import jax.numpy as jnp
import numpy as np
from jax import lax
from jax.experimental import pallas as pl
from jax.experimental.pallas import tpu as pltpu
from jax.sharding import Mesh, PartitionSpec as P

CAP = 2
LANES = 128
HALF = 64
PP = ("ylo", "x", "core")
EP = ("yhi", "zh", "z8")
CHIPS = ("ylo", "x")
Z = ("zh", "z8")
SPREAD = ("ylo", "x", "core", "yhi")
PARTS = (2, 4, 2, 4, 2, 8)
NAMES = PP + EP
INTERPRET = False

BF = jnp.bfloat16
F32 = jnp.float32


def roll_half(value):
    return pltpu.roll(value, HALF, 1)


def low_lanes(shape):
    return lax.broadcasted_iota(jnp.int32, shape, len(shape) - 1) < HALF


def dot_nn(a, b):
    return lax.dot_general(a, b, (((1,), (0,)), ((), ())), preferred_element_type=F32)


def dot_nt(a, b):
    return lax.dot_general(a, b, (((1,), (1,)), ((), ())), preferred_element_type=F32)


def full(shape):
    return pl.BlockSpec(shape, lambda *_: (0,) * len(shape))


def pack_weights_kernel(place, gate, up, down, out):
    core = place[1]
    width = gate.shape[0]
    g = gate[...].astype(F32)
    u = up[...].astype(F32)
    first = jnp.where(core == 0, g, roll_half(g))
    second = jnp.where(core == 0, roll_half(u), u)
    out[:width, :] = jnp.where(low_lanes(g.shape), first, second).astype(BF)
    for i in range(width // LANES):
        out[width + HALF * i : width + HALF * (i + 1), :] = down[:, LANES * i : LANES * (i + 1)]


def pack_weights(place, w_gate, w_up, w_down, width):
    rows = width + HALF * (width // LANES)
    return pl.pallas_call(
        pack_weights_kernel,
        grid_spec=pltpu.PrefetchScalarGridSpec(
            num_scalar_prefetch=1,
            grid=(1,),
            in_specs=[
                pl.BlockSpec((width, LANES), lambda i, s: (s[0], 0)),
                pl.BlockSpec((width, LANES), lambda i, s: (s[0], 0)),
                pl.BlockSpec((HALF, width), lambda i, s: (s[1], s[0])),
            ],
            out_specs=pl.BlockSpec((rows, LANES), lambda i, s: (0, 0)),
        ),
        out_shape=jax.ShapeDtypeStruct((rows, LANES), BF),
        interpret=INTERPRET,
        name="pack_weights",
    )(place, w_gate, w_up, w_down)


def down_pair(weights, width):
    tiles = []
    for i in range(width // LANES):
        lo = width + HALF * i
        tiles.append(jnp.concatenate([weights[0, lo : lo + HALF], weights[1, lo : lo + HALF]], axis=0))
    return jnp.concatenate(tiles, axis=1)


def first_matmul_kernel(rows, weights, out):
    width = rows.shape[3]
    fwd = rows[0, 0]
    bwd = rows[1, 0]
    pair = jnp.concatenate([weights[0, :width], weights[1, :width]], axis=1)
    pre = dot_nn(fwd, pair).astype(BF)
    grad = dot_nt(bwd, down_pair(weights, width)).astype(BF)
    count = out.shape[2]
    for chip in range(out.shape[0]):
        out[chip, 0, :, : 2 * LANES] = pre[chip * count : (chip + 1) * count]
        out[chip, 0, :, 2 * LANES :] = grad[chip * count : (chip + 1) * count]


def first_matmul(rows, weights, chips):
    _, halves, count, width = rows.shape
    pairs = weights.shape[0] // halves // 2
    return pl.pallas_call(
        first_matmul_kernel,
        grid=(halves, pairs),
        in_specs=[
            pl.BlockSpec((2, 1, count, width), lambda h, j: (0, h, 0, 0)),
            pl.BlockSpec((2,) + weights.shape[1:], lambda h, j: (h * pairs + j, 0, 0)),
        ],
        out_specs=pl.BlockSpec((chips, 1, count // chips, 3 * LANES), lambda h, j: (0, h, 0, j)),
        out_shape=jax.ShapeDtypeStruct((chips, halves, count // chips, pairs * 3 * LANES), BF),
        interpret=INTERPRET,
        name="first_matmul",
    )(rows, weights)


def activate_kernel(parts, gates, ups, out):
    chips = parts.shape[0]
    for h in range(parts.shape[1]):
        total = parts[0, h].astype(F32)
        for chip in range(1, chips):
            total = total + parts[chip, h].astype(F32)
        for j in range(parts.shape[3] // (3 * LANES)):
            at = 3 * LANES * j
            hidden = []
            for k in range(2):
                v = total[:, at + LANES * k : at + LANES * (k + 1)]
                hidden.append(v / (1.0 + jnp.exp(-v)) * roll_half(v))
            low = low_lanes(hidden[0].shape)
            hid = jnp.where(low, hidden[0], roll_half(hidden[1]))
            grad = total[:, at + 2 * LANES : at + 3 * LANES]
            gate = gates[h, :, LANES * j : LANES * (j + 1)]
            up = ups[h, :, LANES * j : LANES * (j + 1)]
            sigma = 1.0 / (1.0 + jnp.exp(-gate))
            grad_gate = grad * up * sigma * (1.0 + gate * (1.0 - sigma))
            grad_up = grad * gate * sigma
            tile = jnp.concatenate(
                [
                    jnp.where(low, grad_gate, roll_half(grad_up)),
                    jnp.where(low, roll_half(grad_gate), grad_up),
                    hid,
                ],
                axis=1,
            ).astype(BF)
            for chip in range(chips):
                out[chip, h, :, at : at + 3 * LANES] = tile


def activate(parts, gates, ups):
    return pl.pallas_call(
        activate_kernel,
        out_shape=jax.ShapeDtypeStruct(parts.shape, BF),
        interpret=INTERPRET,
        name="activate",
    )(parts, gates, ups)


def second_matmul_kernel(half, hidden, weights, out, acc):
    width = acc.shape[2]
    chips = hidden.shape[0]
    step = pl.program_id(0)
    rows = jnp.concatenate([hidden[chip, 0] for chip in range(chips)], axis=0)
    fwd = dot_nn(rows[:, 2 * LANES :], down_pair(weights, width))
    pair = jnp.concatenate([weights[0, :width], weights[1, :width]], axis=1)
    bwd = dot_nt(rows[:, : 2 * LANES], pair)

    @pl.when(step == 0)
    def _():
        acc[0] = fwd
        acc[1] = bwd

    @pl.when(step > 0)
    def _():
        acc[0] = acc[0] + fwd
        acc[1] = acc[1] + bwd

    @pl.when(step == pl.num_programs(0) - 1)
    def _():
        out[...] = acc[...].astype(out.dtype)


def second_matmul(half, hidden, weights, width, dtype):
    chips, halves, per_chip, cols = hidden.shape
    pairs = weights.shape[0] // halves // 2
    count = chips * per_chip
    return pl.pallas_call(
        second_matmul_kernel,
        grid_spec=pltpu.PrefetchScalarGridSpec(
            num_scalar_prefetch=1,
            grid=(pairs,),
            in_specs=[
                pl.BlockSpec((chips, 1, per_chip, 3 * LANES), lambda j, s: (0, s[0], 0, j)),
                pl.BlockSpec((2,) + weights.shape[1:], lambda j, s: (s[0] * pairs + j, 0, 0)),
            ],
            out_specs=pl.BlockSpec((2, count, width), lambda j, s: (0, 0, 0)),
            scratch_shapes=[pltpu.VMEM((2, count, width), F32)],
        ),
        out_shape=jax.ShapeDtypeStruct((2, count, width), dtype),
        interpret=INTERPRET,
        name="second_matmul",
    )(half, hidden, weights)


def merge_kernel(kept, other, order, out):
    count = kept.shape[1]
    total = (kept[...] + other[...].astype(F32)).astype(BF)
    out[...] = dot_nn(order[...], total.reshape(2 * count, total.shape[2])).astype(BF)


def merge(kept, other, order):
    _, count, width = kept.shape
    return pl.pallas_call(
        merge_kernel,
        out_shape=jax.ShapeDtypeStruct((2 * count, width), BF),
        interpret=INTERPRET,
        name="merge",
    )(kept, other, order)


def combine_kernel(weight, rows, out):
    w = weight[...]
    top = w.astype(BF)
    rest = w - top.astype(F32)
    mid = rest.astype(BF)
    low = (rest - mid.astype(F32)).astype(BF)
    values = rows[0]
    out[...] = (dot_nn(top, values) + (dot_nn(mid, values) + dot_nn(low, values))).astype(BF)


def combine(weight, rows):
    chips, depth, width = rows.shape
    tokens = weight.shape[0]
    return pl.pallas_call(
        combine_kernel,
        grid=(chips,),
        in_specs=[full(weight.shape), pl.BlockSpec((1, depth, width), lambda q: (q, 0, 0))],
        out_specs=pl.BlockSpec((tokens, width), lambda q: (0, q)),
        out_shape=jax.ShapeDtypeStruct((tokens, chips * width), BF),
        interpret=INTERPRET,
        name="combine",
    )(weight, rows)


def section_order(sections, blocks):
    count = sections * blocks * CAP
    order = np.zeros((sections, blocks, 2, CAP, 2 * count), np.float32)
    for p in range(sections):
        for y in range(blocks):
            for slot in range(CAP):
                for way, source in ((0, (p - 1) % sections), (1, (p + 1) % sections)):
                    order[p, y, way, slot, way * count + (source * blocks + y) * CAP + slot] = 1.0
    return order.reshape(2 * count, 2 * count)


def route_tables(routes, scores, groups):
    experts = jnp.arange(groups, dtype=jnp.int32)
    match = (routes[:, :, None] == experts).astype(F32)
    weight = 2.5 * scores / jnp.sum(scores, axis=-1, keepdims=True)
    hits = jnp.sum(match, axis=1)
    shares = jnp.sum(match * weight[:, :, None], axis=1)
    before = jnp.cumsum(hits, axis=0) - hits
    slots = jnp.arange(CAP, dtype=F32)
    placed = hits[:, :, None] * (before[:, :, None] == slots).astype(F32)
    return (placed, placed * shares[:, :, None])


def gather_rows(values, placed):
    return jnp.einsum(
        "tgc,td->gcd", placed.astype(BF), values, preferred_element_type=F32
    ).astype(BF)


def shifted(value, steps):
    count = lax.axis_size(PP)
    pairs = [(source, (source + steps) % count) for source in range(count)]
    return lax.ppermute(value, PP, pairs)


def all_to_all(value, axes):
    return lax.all_to_all(value, axes, split_axis=0, concat_axis=0, tiled=True)


def body(
    x_fwd, dy_bwd, routes_fwd, routes_bwd, score_fwd, score_bwd, saved_bwd, w_gate, w_up, w_down
):
    chips = lax.axis_size(CHIPS)
    sections = lax.axis_size(PP)
    ny = lax.axis_size("yhi")
    ns = lax.axis_size("z8")
    nz = lax.axis_size(Z)
    groups = 2 * ny
    width = w_gate.shape[0] // chips
    tokens = x_fwd.shape[1]
    core = lax.axis_index("core")
    place = jnp.stack([lax.axis_index(CHIPS), core]).astype(jnp.int32)

    packed = pack_weights(place, w_gate, w_up, w_down, width)
    weights = lax.all_gather(packed, Z, axis=0, tiled=True)
    weights = weights.reshape(nz, packed.shape[0], LANES)

    placed_f, weighted_f = route_tables(routes_fwd[0], score_fwd[0], groups)
    placed_b, weighted_b = route_tables(routes_bwd[0], score_bwd[0], groups)
    rows = jnp.stack([gather_rows(x_fwd[0], placed_f), gather_rows(dy_bwd[0], placed_b)])
    rows = rows.reshape(2, ny, 2, CAP, chips, width).transpose(4, 1, 0, 2, 3, 5)
    rows = jnp.broadcast_to(rows[:, None], (chips, 2) + rows.shape[1:])
    rows = all_to_all(rows.reshape(sections * ny, 4 * CAP, width), SPREAD)
    rows = rows.reshape(sections * ny, 2, 2, CAP, width).transpose(1, 2, 0, 3, 4)
    rows = rows.reshape(2, 2, sections * ny * CAP, width)

    saved = saved_bwd[0].reshape(ny, nz, CAP, 2, 2, HALF).transpose(4, 1, 0, 2, 3, 5)
    saved = all_to_all(saved.reshape(2 * nz, ny * CAP, LANES), ("core",) + Z)
    saved = saved.reshape(2, 2, ns, ny, CAP, 2, HALF).transpose(5, 1, 0, 3, 4, 2, 6)
    saved = saved.reshape(2, 2, 2 * ny * CAP, ns * HALF)

    mix_f = shifted(weighted_f.reshape(tokens, groups * CAP), 1)
    mix_b = shifted(weighted_b.reshape(tokens, groups * CAP), -1)
    mix = jnp.stack([mix_f, mix_b], axis=1).reshape(tokens, 2, ny, 2, CAP).transpose(0, 3, 2, 1, 4)
    mix = mix.reshape(tokens, 4 * ny * CAP)

    parts = all_to_all(first_matmul(rows, weights, chips), CHIPS)
    hidden = all_to_all(activate(parts, saved[0], saved[1]), CHIPS)

    swap = [(0, 1), (1, 0)]
    away = (1 - core).astype(jnp.int32).reshape(1)
    sent = second_matmul(away, hidden, weights, width, BF)
    other = lax.ppermute(sent, "core", swap)
    kept = second_matmul(1 - away, hidden, weights, width, F32)
    order = jnp.asarray(section_order(sections, ny), BF)
    merged = merge(kept, other, order)
    merged = all_to_all(merged.reshape(sections * ny, 2 * CAP, width), SPREAD)
    return combine(mix, merged.reshape(chips, 4 * ny * CAP, width))[None]


def solution(mesh):
    fine = Mesh(mesh.devices.reshape(PARTS), NAMES)
    by_token = P(PP, EP, None)
    in_specs = (by_token,) * 6 + (
        P(PP, None, None, None, EP),
        P(None, EP),
        P(None, EP),
        P(EP, None),
    )
    return jax.shard_map(
        body, mesh=fine, in_specs=in_specs, out_specs=by_token, check_vma=False
    )
```

```python
import functools

import jax
import jax.numpy as jnp
import numpy as np
from jax import lax
from jax.experimental import pallas as pl
from jax.experimental.pallas import tpu as pltpu
from jax.sharding import Mesh, PartitionSpec as P

CAP = 2
LANES = 128
HALF = 64
PP = ("ylo", "x", "core")
EP = ("yhi", "zh", "z8")
CHIPS = ("ylo", "x")
Z = ("zh", "z8")
SPREAD = ("ylo", "x", "core", "yhi")
PARTS = (2, 4, 2, 4, 2, 8)
NAMES = PP + EP
INTERPRET = False

BF = jnp.bfloat16
F32 = jnp.float32


def roll_half(value):
    return pltpu.roll(value, HALF, 1)


def low_lanes(shape):
    return lax.broadcasted_iota(jnp.int32, shape, len(shape) - 1) < HALF


def dot_nn(a, b):
    return lax.dot_general(a, b, (((1,), (0,)), ((), ())), preferred_element_type=F32)


def dot_nt(a, b):
    return lax.dot_general(a, b, (((1,), (1,)), ((), ())), preferred_element_type=F32)


def full(shape):
    return pl.BlockSpec(shape, lambda *_: (0,) * len(shape))


def pack_weights_kernel(place, gate, up, down, mine, other):
    first = place[1] == 0
    width = gate.shape[0]
    g = gate[...].astype(F32)
    u = up[...].astype(F32)
    low = low_lanes(g.shape)
    top = jnp.where(low, g, roll_half(u))
    bottom = jnp.where(low, roll_half(g), u)
    mine[:width, :] = jnp.where(first, top, bottom).astype(BF)
    other[:width, :] = jnp.where(first, bottom, top).astype(BF)
    for i in range(width // LANES):
        at = width + HALF * i
        d_top = down[:HALF, LANES * i : LANES * (i + 1)].astype(F32)
        d_bottom = down[HALF:, LANES * i : LANES * (i + 1)].astype(F32)
        mine[at : at + HALF, :] = jnp.where(first, d_top, d_bottom).astype(BF)
        other[at : at + HALF, :] = jnp.where(first, d_bottom, d_top).astype(BF)


def pack_weights(place, w_gate, w_up, w_down, width):
    rows = width + HALF * (width // LANES)
    return pl.pallas_call(
        pack_weights_kernel,
        grid_spec=pltpu.PrefetchScalarGridSpec(
            num_scalar_prefetch=1,
            grid=(1,),
            in_specs=[
                pl.BlockSpec((width, LANES), lambda i, s: (s[0], 0)),
                pl.BlockSpec((width, LANES), lambda i, s: (s[0], 0)),
                pl.BlockSpec((2 * HALF, width), lambda i, s: (0, s[0])),
            ],
            out_specs=[pl.BlockSpec((rows, LANES), lambda i, s: (0, 0))] * 2,
        ),
        out_shape=[jax.ShapeDtypeStruct((rows, LANES), BF)] * 2,
        interpret=INTERPRET,
        name="pack_weights",
    )(place, w_gate, w_up, w_down)


def gather_over_z(mine, other, nz):
    flows = [(z, (z + 1) % nz) for z in range(nz)]
    flows += [(nz + z, nz + (z - 1) % nz) for z in range(nz)]
    swap = [(0, 1), (1, 0)]
    half = nz // 2
    blocks = jnp.zeros((nz,) + mine.shape, mine.dtype)
    blocks = blocks.at[half].set(mine)
    for step in range(1, half + 1):
        mine = lax.ppermute(mine, ("core",) + Z, flows)
        blocks = blocks.at[half - step].set(mine)
        if step < half:
            other = lax.ppermute(other, ("core",) + Z, flows)
            blocks = blocks.at[half + step].set(lax.ppermute(other, "core", swap))
    return blocks


def down_pair(even, odd, width):
    tiles = []
    for i in range(width // LANES):
        lo = width + HALF * i
        tiles.append(jnp.concatenate([even[0, lo : lo + HALF], odd[0, lo : lo + HALF]], axis=0))
    return jnp.concatenate(tiles, axis=1)


def first_matmul_kernel(table, rows, even, odd, out):
    width = rows.shape[3]
    fwd = rows[0, 0]
    bwd = rows[1, 0]
    pair = jnp.concatenate([even[0, :width], odd[0, :width]], axis=1)
    pre = dot_nn(fwd, pair).astype(BF)
    grad = dot_nt(bwd, down_pair(even, odd, width)).astype(BF)
    count = out.shape[2]
    for chip in range(out.shape[0]):
        out[chip, 0, :, : 2 * LANES] = pre[chip * count : (chip + 1) * count]
        out[chip, 0, :, 2 * LANES :] = grad[chip * count : (chip + 1) * count]


def first_matmul(table, rows, weights, chips):
    _, halves, count, width = rows.shape
    slices = weights.shape[0] // halves
    block = (1,) + weights.shape[1:]
    return pl.pallas_call(
        first_matmul_kernel,
        grid_spec=pltpu.PrefetchScalarGridSpec(
            num_scalar_prefetch=1,
            grid=(halves, slices // 2),
            in_specs=[
                pl.BlockSpec((2, 1, count, width), lambda h, j, s: (0, h, 0, 0)),
                pl.BlockSpec(block, lambda h, j, s: (s[h * slices + 2 * j], 0, 0)),
                pl.BlockSpec(block, lambda h, j, s: (s[h * slices + 2 * j + 1], 0, 0)),
            ],
            out_specs=pl.BlockSpec(
                (chips, 1, count // chips, 3 * LANES), lambda h, j, s: (0, h, 0, j)
            ),
        ),
        out_shape=jax.ShapeDtypeStruct(
            (chips, halves, count // chips, slices // 2 * 3 * LANES), BF
        ),
        interpret=INTERPRET,
        name="first_matmul",
    )(table, rows, weights, weights)


def activate_kernel(parts, gates, ups, out):
    chips = parts.shape[0]
    for h in range(parts.shape[1]):
        total = parts[0, h].astype(F32)
        for chip in range(1, chips):
            total = total + parts[chip, h].astype(F32)
        for j in range(parts.shape[3] // (3 * LANES)):
            at = 3 * LANES * j
            hidden = []
            for k in range(2):
                v = total[:, at + LANES * k : at + LANES * (k + 1)]
                hidden.append(v / (1.0 + jnp.exp(-v)) * roll_half(v))
            low = low_lanes(hidden[0].shape)
            hid = jnp.where(low, hidden[0], roll_half(hidden[1]))
            grad = total[:, at + 2 * LANES : at + 3 * LANES]
            gate = gates[h, :, LANES * j : LANES * (j + 1)]
            up = ups[h, :, LANES * j : LANES * (j + 1)]
            sigma = 1.0 / (1.0 + jnp.exp(-gate))
            grad_gate = grad * up * sigma * (1.0 + gate * (1.0 - sigma))
            grad_up = grad * gate * sigma
            tile = jnp.concatenate(
                [
                    jnp.where(low, grad_gate, roll_half(grad_up)),
                    jnp.where(low, roll_half(grad_gate), grad_up),
                    hid,
                ],
                axis=1,
            ).astype(BF)
            for chip in range(chips):
                out[chip, h, :, at : at + 3 * LANES] = tile


def activate(parts, gates, ups):
    return pl.pallas_call(
        activate_kernel,
        out_shape=jax.ShapeDtypeStruct(parts.shape, BF),
        interpret=INTERPRET,
        name="activate",
    )(parts, gates, ups)


def second_matmul_kernel(table, hidden, even, odd, out, acc):
    width = acc.shape[2]
    chips = hidden.shape[0]
    step = pl.program_id(0)
    rows = jnp.concatenate([hidden[chip, 0] for chip in range(chips)], axis=0)
    fwd = dot_nn(rows[:, 2 * LANES :], down_pair(even, odd, width))
    pair = jnp.concatenate([even[0, :width], odd[0, :width]], axis=1)
    bwd = dot_nt(rows[:, : 2 * LANES], pair)

    @pl.when(step == 0)
    def _():
        acc[0] = fwd
        acc[1] = bwd

    @pl.when(step > 0)
    def _():
        acc[0] = acc[0] + fwd
        acc[1] = acc[1] + bwd

    @pl.when(step == pl.num_programs(0) - 1)
    def _():
        out[...] = acc[...].astype(out.dtype)


def second_matmul(table, hidden, weights, width, dtype):
    chips, halves, per_chip, cols = hidden.shape
    slices = weights.shape[0] // halves
    count = chips * per_chip
    block = (1,) + weights.shape[1:]
    return pl.pallas_call(
        second_matmul_kernel,
        grid_spec=pltpu.PrefetchScalarGridSpec(
            num_scalar_prefetch=1,
            grid=(slices // 2,),
            in_specs=[
                pl.BlockSpec((chips, 1, per_chip, 3 * LANES), lambda j, s: (0, s[slices], 0, j)),
                pl.BlockSpec(block, lambda j, s: (s[2 * j], 0, 0)),
                pl.BlockSpec(block, lambda j, s: (s[2 * j + 1], 0, 0)),
            ],
            out_specs=pl.BlockSpec((2, count, width), lambda j, s: (0, 0, 0)),
            scratch_shapes=[pltpu.VMEM((2, count, width), F32)],
        ),
        out_shape=jax.ShapeDtypeStruct((2, count, width), dtype),
        interpret=INTERPRET,
        name="second_matmul",
    )(table, hidden, weights, weights)


def merge_kernel(kept, other, order, out):
    count = kept.shape[1]
    total = (kept[...] + other[...].astype(F32)).astype(BF)
    moved = dot_nn(order[...], total.reshape(2 * count, total.shape[2]))
    rows = out.shape[1]
    for i in range(out.shape[0]):
        out[i] = moved[rows * i : rows * (i + 1)].astype(BF)


def merge(kept, other, order):
    _, count, width = kept.shape
    return pl.pallas_call(
        merge_kernel,
        out_shape=jax.ShapeDtypeStruct((count // CAP, 2 * CAP, width), BF),
        interpret=INTERPRET,
        name="merge",
    )(kept, other, order)


def combine_kernel(weight, rows, out):
    w = weight[...]
    top = w.astype(BF)
    rest = w - top.astype(F32)
    mid = rest.astype(BF)
    low = (rest - mid.astype(F32)).astype(BF)
    stacked = jnp.concatenate([top, mid, low], axis=0)
    tokens = w.shape[0]
    width = rows.shape[2]
    for chip in range(rows.shape[0]):
        parts = dot_nn(stacked, rows[chip])
        total = parts[:tokens] + (parts[tokens : 2 * tokens] + parts[2 * tokens :])
        out[:, width * chip : width * (chip + 1)] = total.astype(BF)


def combine(weight, rows):
    chips, depth, width = rows.shape
    tokens = weight.shape[0]
    step = max(1, chips // 2)
    return pl.pallas_call(
        combine_kernel,
        grid=(chips // step,),
        in_specs=[full(weight.shape), pl.BlockSpec((step, depth, width), lambda q: (q, 0, 0))],
        out_specs=pl.BlockSpec((tokens, step * width), lambda q: (0, q)),
        out_shape=jax.ShapeDtypeStruct((tokens, chips * width), BF),
        interpret=INTERPRET,
        name="combine",
    )(weight, rows)


def section_order(sections, blocks):
    count = sections * blocks * CAP
    order = np.zeros((sections, blocks, 2, CAP, 2 * count), np.float32)
    for p in range(sections):
        for y in range(blocks):
            for slot in range(CAP):
                for way, source in ((0, (p - 1) % sections), (1, (p + 1) % sections)):
                    order[p, y, way, slot, way * count + (source * blocks + y) * CAP + slot] = 1.0
    return order.reshape(2 * count, 2 * count)


def route_tables(routes, scores, groups):
    experts = jnp.arange(groups, dtype=jnp.int32)
    match = (routes[:, :, None] == experts).astype(F32)
    weight = 2.5 * scores / jnp.sum(scores, axis=-1, keepdims=True)
    hits = jnp.sum(match, axis=1)
    shares = jnp.sum(match * weight[:, :, None], axis=1)
    before = jnp.cumsum(hits, axis=0) - hits
    slots = jnp.arange(CAP, dtype=F32)
    placed = hits[:, :, None] * (before[:, :, None] == slots).astype(F32)
    return (placed, placed * shares[:, :, None])


def gather_rows(values, placed):
    return jnp.einsum(
        "tgc,td->gcd", placed.astype(BF), values, preferred_element_type=F32
    ).astype(BF)


def shifted(value, steps):
    count = lax.axis_size(PP)
    pairs = [(source, (source + steps) % count) for source in range(count)]
    return lax.ppermute(value, PP, pairs)


def all_to_all(value, axes):
    return lax.all_to_all(value, axes, split_axis=0, concat_axis=0, tiled=True)


def body(
    x_fwd, dy_bwd, routes_fwd, routes_bwd, score_fwd, score_bwd, saved_bwd, w_gate, w_up, w_down
):
    chips = lax.axis_size(CHIPS)
    sections = lax.axis_size(PP)
    ny = lax.axis_size("yhi")
    ns = lax.axis_size("z8")
    nz = lax.axis_size(Z)
    groups = 2 * ny
    width = w_gate.shape[0] // chips
    tokens = x_fwd.shape[1]
    core = lax.axis_index("core")
    place = jnp.stack([lax.axis_index(CHIPS), core]).astype(jnp.int32)

    mine, other = pack_weights(place, w_gate, w_up, w_down, width)
    weights = gather_over_z(mine, other, nz)
    ahead = jnp.arange(nz, dtype=jnp.int32) - lax.axis_index(Z)
    table = (nz // 2 + jnp.where(core == 0, ahead, -ahead)) % nz

    placed_f, weighted_f = route_tables(routes_fwd[0], score_fwd[0], groups)
    placed_b, weighted_b = route_tables(routes_bwd[0], score_bwd[0], groups)
    rows = jnp.stack([gather_rows(x_fwd[0], placed_f), gather_rows(dy_bwd[0], placed_b)])
    rows = rows.reshape(2, ny, 2, CAP, chips, width).transpose(4, 1, 0, 2, 3, 5)
    rows = jnp.broadcast_to(rows[:, None], (chips, 2) + rows.shape[1:])
    rows = all_to_all(rows.reshape(sections * ny, 4 * CAP, width), SPREAD)
    rows = rows.reshape(sections * ny, 2, 2, CAP, width).transpose(1, 2, 0, 3, 4)
    rows = rows.reshape(2, 2, sections * ny * CAP, width)

    saved = saved_bwd[0].reshape(ny, nz, CAP, 2, 2, HALF).transpose(4, 1, 0, 2, 3, 5)
    saved = all_to_all(saved.reshape(2 * nz, ny * CAP, LANES), ("core",) + Z)
    saved = saved.reshape(2, 2, ns, ny, CAP, 2, HALF).transpose(5, 1, 0, 3, 4, 2, 6)
    saved = saved.reshape(2, 2, 2 * ny * CAP, ns * HALF)

    mix_f = shifted(weighted_f.reshape(tokens, groups * CAP), 1)
    mix_b = shifted(weighted_b.reshape(tokens, groups * CAP), -1)
    mix = jnp.stack([mix_f, mix_b], axis=1).reshape(tokens, 2, ny, 2, CAP).transpose(0, 3, 2, 1, 4)
    mix = mix.reshape(tokens, 4 * ny * CAP)
    rows, saved, mix = lax.optimization_barrier((rows, saved, mix))

    parts = all_to_all(first_matmul(table, rows, weights, chips), CHIPS)
    hidden = all_to_all(activate(parts, saved[0], saved[1]), CHIPS)

    ours = jnp.where(core == 0, table[:ns], table[ns:])
    theirs = jnp.where(core == 0, table[ns:], table[:ns])
    here = core.astype(jnp.int32).reshape(1)
    sent = second_matmul(jnp.concatenate([theirs, 1 - here]), hidden, weights, width, BF)
    other = lax.ppermute(sent, "core", [(0, 1), (1, 0)])
    kept = second_matmul(jnp.concatenate([ours, here]), hidden, weights, width, F32)
    order = jnp.asarray(section_order(sections, ny), BF)
    merged = merge(kept, other, order)
    merged = all_to_all(merged, SPREAD)
    return combine(mix, merged.reshape(chips, 4 * ny * CAP, width))[None]


def solution(mesh):
    fine = Mesh(mesh.devices.reshape(PARTS), NAMES)
    by_token = P(PP, EP, None)
    in_specs = (by_token,) * 6 + (
        P(PP, None, None, None, EP),
        P(None, EP),
        P(None, EP),
        P(EP, None),
    )
    return jax.shard_map(
        body, mesh=fine, in_specs=in_specs, out_specs=by_token, check_vma=False
    )
```

```python
import functools

import jax
import jax.numpy as jnp
import numpy as np
from jax import lax
from jax.experimental import pallas as pl
from jax.experimental.pallas import tpu as pltpu
from jax.sharding import Mesh, PartitionSpec as P

CAP = 2
LANES = 128
HALF = 64
PP = ("ylo", "x", "core")
EP = ("yhi", "zh", "z8")
CHIPS = ("ylo", "x")
Z = ("zh", "z8")
SPREAD = ("ylo", "x", "core", "yhi")
PARTS = (2, 4, 2, 4, 2, 8)
NAMES = PP + EP
INTERPRET = False
PAIRS = 2

BF = jnp.bfloat16
F32 = jnp.float32


def roll_half(value):
    return pltpu.roll(value, HALF, 1)


def low_lanes(shape):
    return lax.broadcasted_iota(jnp.int32, shape, len(shape) - 1) < HALF


def dot_nn(a, b):
    return lax.dot_general(a, b, (((1,), (0,)), ((), ())), preferred_element_type=F32)


def dot_nt(a, b):
    return lax.dot_general(a, b, (((1,), (1,)), ((), ())), preferred_element_type=F32)


def full(shape):
    return pl.BlockSpec(shape, lambda *_: (0,) * len(shape))


def pack_weights_kernel(place, gate, up, down, out):
    first = place[1] == 0
    width = gate.shape[0]
    g = gate[...].astype(F32)
    u = up[...].astype(F32)
    low = low_lanes(g.shape)
    top = jnp.where(low, g, roll_half(u))
    bottom = jnp.where(low, roll_half(g), u)
    out[:width, :] = jnp.where(first, top, bottom).astype(BF)
    for i in range(width // LANES):
        out[width + HALF * i : width + HALF * (i + 1), :] = down[:, LANES * i : LANES * (i + 1)]


def pack_weights(place, w_gate, w_up, w_down, width):
    rows = width + HALF * (width // LANES)
    return pl.pallas_call(
        pack_weights_kernel,
        grid_spec=pltpu.PrefetchScalarGridSpec(
            num_scalar_prefetch=1,
            grid=(1,),
            in_specs=[
                pl.BlockSpec((width, LANES), lambda i, s: (s[0], 0)),
                pl.BlockSpec((width, LANES), lambda i, s: (s[0], 0)),
                pl.BlockSpec((HALF, width), lambda i, s: (s[1], s[0])),
            ],
            out_specs=pl.BlockSpec((rows, LANES), lambda i, s: (0, 0)),
        ),
        out_shape=jax.ShapeDtypeStruct((rows, LANES), BF),
        interpret=INTERPRET,
        name="pack_weights",
    )(place, w_gate, w_up, w_down)


def down_pair(weights, at, width):
    tiles = []
    for i in range(width // LANES):
        lo = width + HALF * i
        tiles.append(
            jnp.concatenate([weights[at, lo : lo + HALF], weights[at + 1, lo : lo + HALF]], axis=0)
        )
    return jnp.concatenate(tiles, axis=1)


def first_matmul_kernel(rows, weights, out):
    width = rows.shape[3]
    fwd = rows[0, 0]
    bwd = rows[1, 0]
    count = out.shape[2]
    for j in range(weights.shape[0] // 2):
        pair = jnp.concatenate([weights[2 * j, :width], weights[2 * j + 1, :width]], axis=1)
        pre = dot_nn(fwd, pair).astype(BF)
        grad = dot_nt(bwd, down_pair(weights, 2 * j, width)).astype(BF)
        at = 3 * LANES * j
        for chip in range(out.shape[0]):
            span = slice(chip * count, (chip + 1) * count)
            out[chip, 0, :, at : at + 2 * LANES] = pre[span]
            out[chip, 0, :, at + 2 * LANES : at + 3 * LANES] = grad[span]


def first_matmul(rows, weights, chips):
    _, halves, count, width = rows.shape
    pairs = weights.shape[0] // halves // 2
    step = min(PAIRS, pairs)
    return pl.pallas_call(
        first_matmul_kernel,
        grid=(halves, pairs // step),
        in_specs=[
            pl.BlockSpec((2, 1, count, width), lambda h, j: (0, h, 0, 0)),
            pl.BlockSpec(
                (2 * step,) + weights.shape[1:], lambda h, j: (h * (pairs // step) + j, 0, 0)
            ),
        ],
        out_specs=pl.BlockSpec(
            (chips, 1, count // chips, step * 3 * LANES), lambda h, j: (0, h, 0, j)
        ),
        out_shape=jax.ShapeDtypeStruct((chips, halves, count // chips, pairs * 3 * LANES), BF),
        interpret=INTERPRET,
        name="first_matmul",
    )(rows, weights)


def activate_kernel(parts, gates, ups, out):
    chips = parts.shape[0]
    for h in range(parts.shape[1]):
        total = parts[0, h].astype(F32)
        for chip in range(1, chips):
            total = total + parts[chip, h].astype(F32)
        for j in range(parts.shape[3] // (3 * LANES)):
            at = 3 * LANES * j
            hidden = []
            for k in range(2):
                v = total[:, at + LANES * k : at + LANES * (k + 1)]
                hidden.append(v / (1.0 + jnp.exp(-v)) * roll_half(v))
            low = low_lanes(hidden[0].shape)
            hid = jnp.where(low, hidden[0], roll_half(hidden[1]))
            grad = total[:, at + 2 * LANES : at + 3 * LANES]
            gate = gates[h, :, LANES * j : LANES * (j + 1)]
            up = ups[h, :, LANES * j : LANES * (j + 1)]
            sigma = 1.0 / (1.0 + jnp.exp(-gate))
            grad_gate = grad * up * sigma * (1.0 + gate * (1.0 - sigma))
            grad_up = grad * gate * sigma
            tile = jnp.concatenate(
                [
                    jnp.where(low, grad_gate, roll_half(grad_up)),
                    jnp.where(low, roll_half(grad_gate), grad_up),
                    hid,
                ],
                axis=1,
            ).astype(BF)
            for chip in range(chips):
                out[chip, h, :, at : at + 3 * LANES] = tile


def activate(parts, gates, ups):
    return pl.pallas_call(
        activate_kernel,
        out_shape=jax.ShapeDtypeStruct(parts.shape, BF),
        interpret=INTERPRET,
        name="activate",
    )(parts, gates, ups)


def second_matmul_kernel(half, hidden, weights, out, acc):
    width = acc.shape[2]
    chips = hidden.shape[0]
    step = pl.program_id(0)
    rows = jnp.concatenate([hidden[chip, 0] for chip in range(chips)], axis=0)
    pairs = weights.shape[0] // 2
    hid = [rows[:, 3 * LANES * j + 2 * LANES : 3 * LANES * (j + 1)] for j in range(pairs)]
    down = [down_pair(weights, 2 * j, width) for j in range(pairs)]
    fwd = dot_nn(jnp.concatenate(hid, axis=1), jnp.concatenate(down, axis=0))
    grads = [rows[:, 3 * LANES * j : 3 * LANES * j + 2 * LANES] for j in range(pairs)]
    both = jnp.concatenate([weights[j, :width] for j in range(2 * pairs)], axis=1)
    bwd = dot_nt(jnp.concatenate(grads, axis=1), both)

    @pl.when(step == 0)
    def _():
        acc[0] = fwd
        acc[1] = bwd

    @pl.when(step > 0)
    def _():
        acc[0] = acc[0] + fwd
        acc[1] = acc[1] + bwd

    @pl.when(step == pl.num_programs(0) - 1)
    def _():
        out[...] = acc[...].astype(out.dtype)


def second_matmul(half, hidden, weights, width, dtype):
    chips, halves, per_chip, cols = hidden.shape
    pairs = weights.shape[0] // halves // 2
    step = min(PAIRS, pairs)
    count = chips * per_chip
    return pl.pallas_call(
        second_matmul_kernel,
        grid_spec=pltpu.PrefetchScalarGridSpec(
            num_scalar_prefetch=1,
            grid=(pairs // step,),
            in_specs=[
                pl.BlockSpec(
                    (chips, 1, per_chip, step * 3 * LANES), lambda j, s: (0, s[0], 0, j)
                ),
                pl.BlockSpec(
                    (2 * step,) + weights.shape[1:],
                    lambda j, s: (s[0] * (pairs // step) + j, 0, 0),
                ),
            ],
            out_specs=pl.BlockSpec((2, count, width), lambda j, s: (0, 0, 0)),
            scratch_shapes=[pltpu.VMEM((2, count, width), F32)],
        ),
        out_shape=jax.ShapeDtypeStruct((2, count, width), dtype),
        interpret=INTERPRET,
        name="second_matmul",
    )(half, hidden, weights)


def merge_kernel(kept, other, order, out):
    count = kept.shape[1]
    total = (kept[...] + other[...].astype(F32)).astype(BF)
    moved = dot_nn(order[...], total.reshape(2 * count, total.shape[2]))
    rows = out.shape[1]
    for i in range(out.shape[0]):
        out[i] = moved[rows * i : rows * (i + 1)].astype(BF)


def merge(kept, other, order):
    _, count, width = kept.shape
    return pl.pallas_call(
        merge_kernel,
        out_shape=jax.ShapeDtypeStruct((count // CAP, 2 * CAP, width), BF),
        interpret=INTERPRET,
        name="merge",
    )(kept, other, order)


def combine_kernel(weight, rows, out):
    w = weight[...]
    top = w.astype(BF)
    rest = w - top.astype(F32)
    mid = rest.astype(BF)
    low = (rest - mid.astype(F32)).astype(BF)
    stacked = jnp.concatenate([top, mid, low], axis=0)
    tokens = w.shape[0]
    width = rows.shape[2]
    for chip in range(rows.shape[0]):
        parts = dot_nn(stacked, rows[chip])
        total = parts[:tokens] + (parts[tokens : 2 * tokens] + parts[2 * tokens :])
        out[:, width * chip : width * (chip + 1)] = total.astype(BF)


def combine(weight, rows):
    chips, depth, width = rows.shape
    tokens = weight.shape[0]
    step = max(1, chips // 2)
    return pl.pallas_call(
        combine_kernel,
        grid=(chips // step,),
        in_specs=[full(weight.shape), pl.BlockSpec((step, depth, width), lambda q: (q, 0, 0))],
        out_specs=pl.BlockSpec((tokens, step * width), lambda q: (0, q)),
        out_shape=jax.ShapeDtypeStruct((tokens, chips * width), BF),
        interpret=INTERPRET,
        name="combine",
    )(weight, rows)


def section_order(sections, blocks):
    count = sections * blocks * CAP
    order = np.zeros((sections, blocks, 2, CAP, 2 * count), np.float32)
    for p in range(sections):
        for y in range(blocks):
            for slot in range(CAP):
                for way, source in ((0, (p - 1) % sections), (1, (p + 1) % sections)):
                    order[p, y, way, slot, way * count + (source * blocks + y) * CAP + slot] = 1.0
    return order.reshape(2 * count, 2 * count)


def route_tables(routes, scores, groups):
    experts = jnp.arange(groups, dtype=jnp.int32)
    match = (routes[:, :, None] == experts).astype(F32)
    weight = 2.5 * scores / jnp.sum(scores, axis=-1, keepdims=True)
    hits = jnp.sum(match, axis=1)
    shares = jnp.sum(match * weight[:, :, None], axis=1)
    before = jnp.cumsum(hits, axis=0) - hits
    slots = jnp.arange(CAP, dtype=F32)
    placed = hits[:, :, None] * (before[:, :, None] == slots).astype(F32)
    return (placed, placed * shares[:, :, None])


def gather_rows(values, placed):
    return jnp.einsum(
        "tgc,td->gcd", placed.astype(BF), values, preferred_element_type=F32
    ).astype(BF)


def shifted(value, steps):
    count = lax.axis_size(PP)
    pairs = [(source, (source + steps) % count) for source in range(count)]
    return lax.ppermute(value, PP, pairs)


def all_to_all(value, axes):
    return lax.all_to_all(value, axes, split_axis=0, concat_axis=0, tiled=True)


def body(
    x_fwd, dy_bwd, routes_fwd, routes_bwd, score_fwd, score_bwd, saved_bwd, w_gate, w_up, w_down
):
    chips = lax.axis_size(CHIPS)
    sections = lax.axis_size(PP)
    ny = lax.axis_size("yhi")
    ns = lax.axis_size("z8")
    nz = lax.axis_size(Z)
    groups = 2 * ny
    width = w_gate.shape[0] // chips
    tokens = x_fwd.shape[1]
    core = lax.axis_index("core")
    place = jnp.stack([lax.axis_index(CHIPS), core]).astype(jnp.int32)

    packed = pack_weights(place, w_gate, w_up, w_down, width)
    weights = lax.all_gather(packed, Z, axis=0, tiled=True)
    weights = weights.reshape(nz, packed.shape[0], LANES)

    placed_f, weighted_f = route_tables(routes_fwd[0], score_fwd[0], groups)
    placed_b, weighted_b = route_tables(routes_bwd[0], score_bwd[0], groups)
    rows = jnp.stack([gather_rows(x_fwd[0], placed_f), gather_rows(dy_bwd[0], placed_b)])
    rows = rows.reshape(2, ny, 2, CAP, chips, width).transpose(4, 1, 0, 2, 3, 5)
    rows = jnp.broadcast_to(rows[:, None], (chips, 2) + rows.shape[1:])
    rows = all_to_all(rows.reshape(sections * ny, 4 * CAP, width), SPREAD)
    rows = rows.reshape(sections * ny, 2, 2, CAP, width).transpose(1, 2, 0, 3, 4)
    rows = rows.reshape(2, 2, sections * ny * CAP, width)

    saved = saved_bwd[0].reshape(ny, nz, CAP, 2, 2, HALF).transpose(4, 1, 0, 2, 3, 5)
    saved = all_to_all(saved.reshape(2 * nz, ny * CAP, LANES), ("core",) + Z)
    saved = saved.reshape(2, 2, ns, ny, CAP, 2, HALF).transpose(5, 1, 0, 3, 4, 2, 6)
    saved = saved.reshape(2, 2, 2 * ny * CAP, ns * HALF)

    mix_f = shifted(weighted_f.reshape(tokens, groups * CAP), 1)
    mix_b = shifted(weighted_b.reshape(tokens, groups * CAP), -1)
    mix = jnp.stack([mix_f, mix_b], axis=1).reshape(tokens, 2, ny, 2, CAP).transpose(0, 3, 2, 1, 4)
    mix = mix.reshape(tokens, 4 * ny * CAP)
    rows, saved, mix = lax.optimization_barrier((rows, saved, mix))

    parts = all_to_all(first_matmul(rows, weights, chips), CHIPS)
    hidden = all_to_all(activate(parts, saved[0], saved[1]), CHIPS)

    away = (1 - core).astype(jnp.int32).reshape(1)
    sent = second_matmul(away, hidden, weights, width, BF)
    other = lax.ppermute(sent, "core", [(0, 1), (1, 0)])
    kept = second_matmul(1 - away, hidden, weights, width, F32)
    order = jnp.asarray(section_order(sections, ny), BF)
    merged = merge(kept, other, order)
    merged = all_to_all(merged, SPREAD)
    return combine(mix, merged.reshape(chips, 4 * ny * CAP, width))[None]


def solution(mesh):
    fine = Mesh(mesh.devices.reshape(PARTS), NAMES)
    by_token = P(PP, EP, None)
    in_specs = (by_token,) * 6 + (
        P(PP, None, None, None, EP),
        P(None, EP),
        P(None, EP),
        P(EP, None),
    )
    return jax.shard_map(
        body, mesh=fine, in_specs=in_specs, out_specs=by_token, check_vma=False
    )
```

```python
import functools

import jax
import jax.numpy as jnp
import numpy as np
from jax import lax
from jax.experimental import pallas as pl
from jax.experimental.pallas import tpu as pltpu
from jax.sharding import Mesh, PartitionSpec as P

CAP = 2
LANES = 128
HALF = 64
PP = ("ylo", "x", "core")
EP = ("yhi", "zh", "z8")
CHIPS = ("ylo", "x")
Z = ("zh", "z8")
SPREAD = ("ylo", "x", "core", "yhi")
PARTS = (2, 4, 2, 4, 2, 8)
NAMES = PP + EP
INTERPRET = False
PAIRS = 2

BF = jnp.bfloat16
F32 = jnp.float32


def roll_half(value):
    return pltpu.roll(value, HALF, 1)


def low_lanes(shape):
    return lax.broadcasted_iota(jnp.int32, shape, len(shape) - 1) < HALF


def dot_nn(a, b):
    return lax.dot_general(a, b, (((1,), (0,)), ((), ())), preferred_element_type=F32)


def dot_nt(a, b):
    return lax.dot_general(a, b, (((1,), (1,)), ((), ())), preferred_element_type=F32)


def in_vmem(value):
    return value if INTERPRET else pltpu.with_memory_space_constraint(value, pltpu.VMEM)


def in_hbm(value):
    return value if INTERPRET else pltpu.with_memory_space_constraint(value, pltpu.HBM)


SMALL = pltpu.CompilerParams(vmem_limit_bytes=20 << 20)
VMEM_SPEC = pl.BlockSpec(memory_space=pltpu.VMEM)


def full(shape):
    return pl.BlockSpec(shape, lambda *_: (0,) * len(shape))


def pack_weights_kernel(place, gate, up, down, out):
    first = place[1] == 0
    width = gate.shape[0]
    g = gate[...].astype(F32)
    u = up[...].astype(F32)
    low = low_lanes(g.shape)
    top = jnp.where(low, g, roll_half(u))
    bottom = jnp.where(low, roll_half(g), u)
    out[:width, :] = jnp.where(first, top, bottom).astype(BF)
    for i in range(width // LANES):
        out[width + HALF * i : width + HALF * (i + 1), :] = down[:, LANES * i : LANES * (i + 1)]


def pack_weights(place, w_gate, w_up, w_down, width):
    rows = width + HALF * (width // LANES)
    return pl.pallas_call(
        pack_weights_kernel,
        grid_spec=pltpu.PrefetchScalarGridSpec(
            num_scalar_prefetch=1,
            grid=(1,),
            in_specs=[
                pl.BlockSpec((width, LANES), lambda i, s: (s[0], 0)),
                pl.BlockSpec((width, LANES), lambda i, s: (s[0], 0)),
                pl.BlockSpec((HALF, width), lambda i, s: (s[1], s[0])),
            ],
            out_specs=pl.BlockSpec((rows, LANES), lambda i, s: (0, 0)),
        ),
        out_shape=jax.ShapeDtypeStruct((rows, LANES), BF),
        interpret=INTERPRET,
        name="pack_weights",
    )(place, w_gate, w_up, w_down)


def down_pair(weights, at, width):
    tiles = []
    for i in range(width // LANES):
        lo = width + HALF * i
        tiles.append(
            jnp.concatenate([weights[at, lo : lo + HALF], weights[at + 1, lo : lo + HALF]], axis=0)
        )
    return jnp.concatenate(tiles, axis=1)


def first_matmul_kernel(rows, source, out, weights, sems):
    halves, count, width = rows.shape[1:]
    chips = out.shape[0]
    per_chip = count // chips
    total = weights.shape[0]
    copies = [
        pltpu.make_async_copy(source.at[2 * i : 2 * i + 2], weights.at[2 * i : 2 * i + 2], sems.at[i])
        for i in range(total // 2)
    ]
    for copy in copies:
        copy.start()
    for i, copy in enumerate(copies):
        h, j = divmod(i, total // 2 // halves)
        copy.wait()
        pair = jnp.concatenate([weights[2 * i, :width], weights[2 * i + 1, :width]], axis=1)
        pre = dot_nn(rows[0, h], pair).astype(BF)
        grad = dot_nt(rows[1, h], down_pair(weights, 2 * i, width)).astype(BF)
        at = 3 * LANES * j
        for chip in range(chips):
            span = slice(chip * per_chip, (chip + 1) * per_chip)
            out[chip, h, :, at : at + 2 * LANES] = pre[span]
            out[chip, h, :, at + 2 * LANES : at + 3 * LANES] = grad[span]


def first_matmul(rows, weights, chips):
    _, halves, count, _ = rows.shape
    total = weights.shape[0]
    shape = (chips, halves, count // chips, total // halves // 2 * 3 * LANES)
    return pl.pallas_call(
        first_matmul_kernel,
        in_specs=[VMEM_SPEC, pl.BlockSpec(memory_space=pl.ANY)],
        out_specs=VMEM_SPEC,
        out_shape=jax.ShapeDtypeStruct(shape, BF),
        scratch_shapes=[pltpu.VMEM(weights.shape, BF), pltpu.SemaphoreType.DMA((total // 2,))],
        interpret=INTERPRET,
        compiler_params=SMALL,
        name="first_matmul",
    )(in_vmem(rows), in_hbm(weights))


def activate_kernel(parts, gates, ups, out):
    chips = parts.shape[0]
    for h in range(parts.shape[1]):
        total = parts[0, h].astype(F32)
        for chip in range(1, chips):
            total = total + parts[chip, h].astype(F32)
        for j in range(parts.shape[3] // (3 * LANES)):
            at = 3 * LANES * j
            hidden = []
            for k in range(2):
                v = total[:, at + LANES * k : at + LANES * (k + 1)]
                hidden.append(v / (1.0 + jnp.exp(-v)) * roll_half(v))
            low = low_lanes(hidden[0].shape)
            hid = jnp.where(low, hidden[0], roll_half(hidden[1]))
            grad = total[:, at + 2 * LANES : at + 3 * LANES]
            gate = gates[h, :, LANES * j : LANES * (j + 1)].astype(F32)
            up = ups[h, :, LANES * j : LANES * (j + 1)].astype(F32)
            sigma = 1.0 / (1.0 + jnp.exp(-gate))
            grad_gate = grad * up * sigma * (1.0 + gate * (1.0 - sigma))
            grad_up = grad * gate * sigma
            tile = jnp.concatenate(
                [
                    jnp.where(low, grad_gate, roll_half(grad_up)),
                    jnp.where(low, roll_half(grad_gate), grad_up),
                    hid,
                ],
                axis=1,
            ).astype(BF)
            for chip in range(chips):
                out[chip, h, :, at : at + 3 * LANES] = tile


def activate(parts, gates, ups):
    return pl.pallas_call(
        activate_kernel,
        in_specs=[VMEM_SPEC] * 3,
        out_shape=jax.ShapeDtypeStruct(parts.shape, BF),
        interpret=INTERPRET,
        compiler_params=SMALL,
        name="activate",
    )(in_vmem(parts), in_vmem(gates), in_vmem(ups))


def second_matmul_kernel(half, hidden, source, out, weights, sems):
    h = half[0]
    width = out.shape[2]
    slices = weights.shape[0]
    pairs = slices // 2
    copies = [
        pltpu.make_async_copy(
            source.at[pl.ds(slices * h + 2 * j, 2)], weights.at[2 * j : 2 * j + 2], sems.at[j]
        )
        for j in range(pairs)
    ]
    for copy in copies:
        copy.start()
    rows = jnp.concatenate([hidden[chip, h] for chip in range(hidden.shape[0])], axis=0)
    fwd = None
    bwd = None
    for j, copy in enumerate(copies):
        copy.wait()
        at = 3 * LANES * j
        pair = jnp.concatenate([weights[2 * j, :width], weights[2 * j + 1, :width]], axis=1)
        more_f = dot_nn(rows[:, at + 2 * LANES : at + 3 * LANES], down_pair(weights, 2 * j, width))
        more_b = dot_nt(rows[:, at : at + 2 * LANES], pair)
        fwd = more_f if fwd is None else fwd + more_f
        bwd = more_b if bwd is None else bwd + more_b
    out[0] = fwd.astype(out.dtype)
    out[1] = bwd.astype(out.dtype)


def second_matmul(half, hidden, weights, width, dtype):
    chips, halves, per_chip, _ = hidden.shape
    slices = weights.shape[0] // halves
    return pl.pallas_call(
        second_matmul_kernel,
        in_specs=[
            pl.BlockSpec(memory_space=pltpu.SMEM),
            VMEM_SPEC,
            pl.BlockSpec(memory_space=pl.ANY),
        ],
        out_specs=VMEM_SPEC,
        out_shape=jax.ShapeDtypeStruct((2, chips * per_chip, width), dtype),
        scratch_shapes=[
            pltpu.VMEM((slices,) + weights.shape[1:], BF),
            pltpu.SemaphoreType.DMA((slices // 2,)),
        ],
        interpret=INTERPRET,
        compiler_params=SMALL,
        name="second_matmul",
    )(half, in_vmem(hidden), in_hbm(weights))


def merge_kernel(kept, other, order, out):
    count = kept.shape[1]
    total = (kept[...] + other[...].astype(F32)).astype(BF)
    moved = dot_nn(order[...], total.reshape(2 * count, total.shape[2]))
    rows = out.shape[1]
    for i in range(out.shape[0]):
        out[i] = moved[rows * i : rows * (i + 1)].astype(BF)


def merge(kept, other, order):
    _, count, width = kept.shape
    return pl.pallas_call(
        merge_kernel,
        in_specs=[VMEM_SPEC] * 3,
        out_shape=jax.ShapeDtypeStruct((count // CAP, 2 * CAP, width), BF),
        interpret=INTERPRET,
        compiler_params=SMALL,
        name="merge",
    )(in_vmem(kept), in_vmem(other), in_vmem(order))


def combine_kernel(weight, rows, out):
    w = weight[...]
    top = w.astype(BF)
    rest = w - top.astype(F32)
    mid = rest.astype(BF)
    low = (rest - mid.astype(F32)).astype(BF)
    stacked = jnp.concatenate([top, mid, low], axis=0)
    tokens = w.shape[0]
    width = rows.shape[2]
    for chip in range(rows.shape[0]):
        parts = dot_nn(stacked, rows[chip])
        total = parts[:tokens] + (parts[tokens : 2 * tokens] + parts[2 * tokens :])
        out[:, width * chip : width * (chip + 1)] = total.astype(BF)


def combine(weight, rows):
    chips, depth, width = rows.shape
    tokens = weight.shape[0]
    step = max(1, chips // 2)
    return pl.pallas_call(
        combine_kernel,
        grid=(chips // step,),
        in_specs=[full(weight.shape), pl.BlockSpec((step, depth, width), lambda q: (q, 0, 0))],
        out_specs=pl.BlockSpec((tokens, step * width), lambda q: (0, q)),
        out_shape=jax.ShapeDtypeStruct((tokens, chips * width), BF),
        interpret=INTERPRET,
        compiler_params=SMALL,
        name="combine",
    )(weight, in_vmem(rows))


def section_order(sections, blocks):
    count = sections * blocks * CAP
    order = np.zeros((sections, blocks, 2, CAP, 2 * count), np.float32)
    for p in range(sections):
        for y in range(blocks):
            for slot in range(CAP):
                for way, source in ((0, (p - 1) % sections), (1, (p + 1) % sections)):
                    order[p, y, way, slot, way * count + (source * blocks + y) * CAP + slot] = 1.0
    return order.reshape(2 * count, 2 * count)


def route_tables(routes, scores, groups):
    experts = jnp.arange(groups, dtype=jnp.int32)
    match = (routes[:, :, None] == experts).astype(F32)
    weight = 2.5 * scores / jnp.sum(scores, axis=-1, keepdims=True)
    hits = jnp.sum(match, axis=1)
    shares = jnp.sum(match * weight[:, :, None], axis=1)
    before = jnp.cumsum(hits, axis=0) - hits
    slots = jnp.arange(CAP, dtype=F32)
    placed = hits[:, :, None] * (before[:, :, None] == slots).astype(F32)
    return (placed, placed * shares[:, :, None])


def gather_rows(values, placed):
    return jnp.einsum(
        "tgc,td->gcd", placed.astype(BF), values, preferred_element_type=F32
    ).astype(BF)


def shifted(value, steps):
    count = lax.axis_size(PP)
    pairs = [(source, (source + steps) % count) for source in range(count)]
    return lax.ppermute(value, PP, pairs)


def all_to_all(value, axes):
    return lax.all_to_all(value, axes, split_axis=0, concat_axis=0, tiled=True)


def body(
    x_fwd, dy_bwd, routes_fwd, routes_bwd, score_fwd, score_bwd, saved_bwd, w_gate, w_up, w_down
):
    chips = lax.axis_size(CHIPS)
    sections = lax.axis_size(PP)
    ny = lax.axis_size("yhi")
    ns = lax.axis_size("z8")
    nz = lax.axis_size(Z)
    groups = 2 * ny
    width = w_gate.shape[0] // chips
    tokens = x_fwd.shape[1]
    core = lax.axis_index("core")
    place = jnp.stack([lax.axis_index(CHIPS), core]).astype(jnp.int32)

    packed = pack_weights(place, w_gate, w_up, w_down, width)
    weights = lax.all_gather(packed, Z, axis=0, tiled=True)
    weights = weights.reshape(nz, packed.shape[0], LANES)

    placed_f, weighted_f = route_tables(routes_fwd[0], score_fwd[0], groups)
    placed_b, weighted_b = route_tables(routes_bwd[0], score_bwd[0], groups)
    rows = jnp.stack([gather_rows(x_fwd[0], placed_f), gather_rows(dy_bwd[0], placed_b)])
    rows = rows.reshape(2, ny, 2, CAP, chips, width).transpose(4, 1, 0, 2, 3, 5)
    rows = jnp.broadcast_to(rows[:, None], (chips, 2) + rows.shape[1:])
    rows = all_to_all(rows.reshape(sections * ny, 4 * CAP, width), SPREAD)
    rows = rows.reshape(sections * ny, 2, 2, CAP, width).transpose(1, 2, 0, 3, 4)
    rows = rows.reshape(2, 2, sections * ny * CAP, width)

    saved = saved_bwd[0].astype(BF).reshape(ny, nz, CAP, 2, 2, HALF).transpose(4, 1, 0, 2, 3, 5)
    saved = all_to_all(saved.reshape(2 * nz, ny * CAP, LANES), ("core",) + Z)
    saved = saved.reshape(2, 2, ns, ny, CAP, 2, HALF).transpose(5, 1, 0, 3, 4, 2, 6)
    saved = saved.reshape(2, 2, 2 * ny * CAP, ns * HALF)

    mix_f = shifted(weighted_f.reshape(tokens, groups * CAP), 1)
    mix_b = shifted(weighted_b.reshape(tokens, groups * CAP), -1)
    mix = jnp.stack([mix_f, mix_b], axis=1).reshape(tokens, 2, ny, 2, CAP).transpose(0, 3, 2, 1, 4)
    mix = mix.reshape(tokens, 4 * ny * CAP)
    rows, saved, mix = lax.optimization_barrier((rows, saved, mix))

    parts = all_to_all(first_matmul(rows, weights, chips), CHIPS)
    hidden = all_to_all(activate(parts, saved[0], saved[1]), CHIPS)

    away = (1 - core).astype(jnp.int32).reshape(1)
    sent = second_matmul(away, hidden, weights, width, BF)
    other = lax.ppermute(sent, "core", [(0, 1), (1, 0)])
    kept = second_matmul(1 - away, hidden, weights, width, F32)
    order = jnp.asarray(section_order(sections, ny), BF)
    merged = merge(kept, other, order)
    merged = all_to_all(merged, SPREAD)
    return combine(mix, merged.reshape(chips, 4 * ny * CAP, width))[None]


def solution(mesh):
    fine = Mesh(mesh.devices.reshape(PARTS), NAMES)
    by_token = P(PP, EP, None)
    in_specs = (by_token,) * 6 + (
        P(PP, None, None, None, EP),
        P(None, EP),
        P(None, EP),
        P(EP, None),
    )
    return jax.shard_map(
        body, mesh=fine, in_specs=in_specs, out_specs=by_token, check_vma=False
    )
```

```python
import functools

import jax
import jax.numpy as jnp
import numpy as np
from jax import lax
from jax.experimental import pallas as pl
from jax.experimental.pallas import tpu as pltpu
from jax.sharding import Mesh, PartitionSpec as P

CAP = 2
LANES = 128
HALF = 64
PP = ("ylo", "x", "core")
EP = ("yhi", "zh", "z8")
CHIPS = ("ylo", "x")
Z = ("zh", "z8")
SPREAD = ("ylo", "x", "core", "yhi")
PARTS = (2, 4, 2, 4, 2, 8)
NAMES = PP + EP
INTERPRET = False
GROUP = 4

BF = jnp.bfloat16
F32 = jnp.float32


def roll_half(value):
    return pltpu.roll(value, HALF, 1)


def low_lanes(shape):
    return lax.broadcasted_iota(jnp.int32, shape, len(shape) - 1) < HALF


def dot_nn(a, b):
    return lax.dot_general(a, b, (((1,), (0,)), ((), ())), preferred_element_type=F32)


def dot_nt(a, b):
    return lax.dot_general(a, b, (((1,), (1,)), ((), ())), preferred_element_type=F32)


def in_vmem(value):
    return value if INTERPRET else pltpu.with_memory_space_constraint(value, pltpu.VMEM)


def in_hbm(value):
    return value if INTERPRET else pltpu.with_memory_space_constraint(value, pltpu.HBM)


SMALL = pltpu.CompilerParams(vmem_limit_bytes=20 << 20)
VMEM_SPEC = pl.BlockSpec(memory_space=pltpu.VMEM)


def full(shape):
    return pl.BlockSpec(shape, lambda *_: (0,) * len(shape))


def pack_weights_kernel(gate, up, down, out, g_ref, u_ref, d_ref, sems):
    width = g_ref.shape[0]
    chip = lax.axis_index("ylo") * lax.axis_size("x") + lax.axis_index("x")
    core = lax.axis_index("core")
    rows = pl.ds(pl.multiple_of(chip * width, width), width)
    half = pl.ds(pl.multiple_of(core * HALF, HALF), HALF)
    copies = [
        pltpu.make_async_copy(gate.at[rows], g_ref, sems.at[0]),
        pltpu.make_async_copy(up.at[rows], u_ref, sems.at[1]),
        pltpu.make_async_copy(down.at[half, rows], d_ref, sems.at[2]),
    ]
    for copy in copies:
        copy.start()
    for copy in copies:
        copy.wait()
    first = core == 0
    g = g_ref[...].astype(F32)
    u = u_ref[...].astype(F32)
    low = low_lanes(g.shape)
    top = jnp.where(low, g, roll_half(u))
    bottom = jnp.where(low, roll_half(g), u)
    out[:width, :] = jnp.where(first, top, bottom).astype(BF)
    for i in range(width // LANES):
        out[width + HALF * i : width + HALF * (i + 1), :] = d_ref[:, LANES * i : LANES * (i + 1)]


def pack_weights(w_gate, w_up, w_down, width):
    rows = width + HALF * (width // LANES)
    return pl.pallas_call(
        pack_weights_kernel,
        in_specs=[pl.BlockSpec(memory_space=pl.ANY)] * 3,
        out_specs=VMEM_SPEC,
        out_shape=jax.ShapeDtypeStruct((rows, LANES), BF),
        scratch_shapes=[
            pltpu.VMEM((width, LANES), BF),
            pltpu.VMEM((width, LANES), BF),
            pltpu.VMEM((HALF, width), BF),
            pltpu.SemaphoreType.DMA((3,)),
        ],
        interpret=INTERPRET,
        compiler_params=SMALL,
        name="pack_weights",
    )(in_hbm(w_gate), in_hbm(w_up), in_hbm(w_down))


def down_rows(weights, at, count, width):
    tiles = []
    for i in range(width // LANES):
        lo = width + HALF * i
        parts = [weights[at + k, lo : lo + HALF] for k in range(count)]
        tiles.append(jnp.concatenate(parts, axis=0))
    return jnp.concatenate(tiles, axis=1)


def up_columns(weights, at, count, width):
    return jnp.concatenate([weights[at + k, :width] for k in range(count)], axis=1)


def first_matmul_kernel(rows, source, out, weights, sems):
    halves, count, width = rows.shape[1:]
    chips = out.shape[0]
    per_chip = count // chips
    total = weights.shape[0]
    copies = [
        pltpu.make_async_copy(
            source.at[GROUP * i : GROUP * (i + 1)], weights.at[GROUP * i : GROUP * (i + 1)], sems.at[i]
        )
        for i in range(total // GROUP)
    ]
    for copy in copies:
        copy.start()
    for i, copy in enumerate(copies):
        h, j = divmod(i, total // GROUP // halves)
        copy.wait()
        pre = dot_nn(rows[0, h], up_columns(weights, GROUP * i, GROUP, width)).astype(BF)
        grad = dot_nt(rows[1, h], down_rows(weights, GROUP * i, GROUP, width)).astype(BF)
        for chip in range(chips):
            span = slice(chip * per_chip, (chip + 1) * per_chip)
            for k in range(GROUP // 2):
                at = 3 * LANES * (j * GROUP // 2 + k)
                out[chip, h, :, at : at + 2 * LANES] = pre[span, 2 * LANES * k : 2 * LANES * (k + 1)]
                out[chip, h, :, at + 2 * LANES : at + 3 * LANES] = grad[
                    span, LANES * k : LANES * (k + 1)
                ]


def first_matmul(rows, weights, chips):
    _, halves, count, _ = rows.shape
    total = weights.shape[0]
    shape = (chips, halves, count // chips, total // halves // 2 * 3 * LANES)
    return pl.pallas_call(
        first_matmul_kernel,
        in_specs=[VMEM_SPEC, pl.BlockSpec(memory_space=pl.ANY)],
        out_specs=VMEM_SPEC,
        out_shape=jax.ShapeDtypeStruct(shape, BF),
        scratch_shapes=[pltpu.VMEM(weights.shape, BF), pltpu.SemaphoreType.DMA((total // GROUP,))],
        interpret=INTERPRET,
        compiler_params=SMALL,
        name="first_matmul",
    )(in_vmem(rows), in_hbm(weights))


def activate_kernel(parts, gates, ups, out):
    chips = parts.shape[0]
    for h in range(parts.shape[1]):
        total = parts[0, h].astype(F32)
        for chip in range(1, chips):
            total = total + parts[chip, h].astype(F32)
        for j in range(parts.shape[3] // (3 * LANES)):
            at = 3 * LANES * j
            hidden = []
            for k in range(2):
                v = total[:, at + LANES * k : at + LANES * (k + 1)]
                hidden.append(v / (1.0 + jnp.exp(-v)) * roll_half(v))
            low = low_lanes(hidden[0].shape)
            hid = jnp.where(low, hidden[0], roll_half(hidden[1]))
            grad = total[:, at + 2 * LANES : at + 3 * LANES]
            gate = gates[h, :, LANES * j : LANES * (j + 1)].astype(F32)
            up = ups[h, :, LANES * j : LANES * (j + 1)].astype(F32)
            sigma = 1.0 / (1.0 + jnp.exp(-gate))
            grad_gate = grad * up * sigma * (1.0 + gate * (1.0 - sigma))
            grad_up = grad * gate * sigma
            tile = jnp.concatenate(
                [
                    jnp.where(low, grad_gate, roll_half(grad_up)),
                    jnp.where(low, roll_half(grad_gate), grad_up),
                    hid,
                ],
                axis=1,
            ).astype(BF)
            for chip in range(chips):
                out[chip, h, :, at : at + 3 * LANES] = tile


def activate(parts, gates, ups):
    return pl.pallas_call(
        activate_kernel,
        in_specs=[VMEM_SPEC] * 3,
        out_shape=jax.ShapeDtypeStruct(parts.shape, BF),
        interpret=INTERPRET,
        compiler_params=SMALL,
        name="activate",
    )(in_vmem(parts), in_vmem(gates), in_vmem(ups))


def second_matmul_kernel(half, hidden, source, out, weights, sems):
    h = half[0]
    width = out.shape[2]
    slices = weights.shape[0]
    copies = [
        pltpu.make_async_copy(
            source.at[pl.ds(slices * h + GROUP * j, GROUP)],
            weights.at[GROUP * j : GROUP * (j + 1)],
            sems.at[j],
        )
        for j in range(slices // GROUP)
    ]
    for copy in copies:
        copy.start()
    rows = jnp.concatenate([hidden[chip, h] for chip in range(hidden.shape[0])], axis=0)
    fwd = None
    bwd = None
    for j, copy in enumerate(copies):
        copy.wait()
        ats = [3 * LANES * (j * GROUP // 2 + k) for k in range(GROUP // 2)]
        hid = jnp.concatenate([rows[:, at + 2 * LANES : at + 3 * LANES] for at in ats], axis=1)
        grads = jnp.concatenate([rows[:, at : at + 2 * LANES] for at in ats], axis=1)
        more_f = dot_nn(hid, down_rows(weights, GROUP * j, GROUP, width))
        more_b = dot_nt(grads, up_columns(weights, GROUP * j, GROUP, width))
        fwd = more_f if fwd is None else fwd + more_f
        bwd = more_b if bwd is None else bwd + more_b
    out[0] = fwd.astype(out.dtype)
    out[1] = bwd.astype(out.dtype)


def second_matmul(half, hidden, weights, width, dtype):
    chips, halves, per_chip, _ = hidden.shape
    slices = weights.shape[0] // halves
    return pl.pallas_call(
        second_matmul_kernel,
        in_specs=[
            pl.BlockSpec(memory_space=pltpu.SMEM),
            VMEM_SPEC,
            pl.BlockSpec(memory_space=pl.ANY),
        ],
        out_specs=VMEM_SPEC,
        out_shape=jax.ShapeDtypeStruct((2, chips * per_chip, width), dtype),
        scratch_shapes=[
            pltpu.VMEM((slices,) + weights.shape[1:], BF),
            pltpu.SemaphoreType.DMA((slices // GROUP,)),
        ],
        interpret=INTERPRET,
        compiler_params=SMALL,
        name="second_matmul",
    )(half, in_vmem(hidden), in_hbm(weights))


def merge_kernel(kept, other, order, out):
    count = kept.shape[1]
    total = (kept[...] + other[...].astype(F32)).astype(BF)
    moved = dot_nn(order[...], total.reshape(2 * count, total.shape[2]))
    rows = out.shape[1]
    for i in range(out.shape[0]):
        out[i] = moved[rows * i : rows * (i + 1)].astype(BF)


def merge(kept, other, order):
    _, count, width = kept.shape
    return pl.pallas_call(
        merge_kernel,
        in_specs=[VMEM_SPEC] * 3,
        out_shape=jax.ShapeDtypeStruct((count // CAP, 2 * CAP, width), BF),
        interpret=INTERPRET,
        compiler_params=SMALL,
        name="merge",
    )(in_vmem(kept), in_vmem(other), in_vmem(order))


def combine_kernel(weight, rows, out):
    w = weight[...]
    top = w.astype(BF)
    rest = w - top.astype(F32)
    mid = rest.astype(BF)
    low = (rest - mid.astype(F32)).astype(BF)
    stacked = jnp.concatenate([top, mid, low], axis=0)
    tokens = w.shape[0]
    width = rows.shape[2]
    for chip in range(rows.shape[0]):
        parts = dot_nn(stacked, rows[chip])
        total = parts[:tokens] + (parts[tokens : 2 * tokens] + parts[2 * tokens :])
        out[:, width * chip : width * (chip + 1)] = total.astype(BF)


def combine(weight, rows):
    chips, depth, width = rows.shape
    tokens = weight.shape[0]
    step = max(1, chips // 2)
    return pl.pallas_call(
        combine_kernel,
        grid=(chips // step,),
        in_specs=[full(weight.shape), pl.BlockSpec((step, depth, width), lambda q: (q, 0, 0))],
        out_specs=pl.BlockSpec((tokens, step * width), lambda q: (0, q)),
        out_shape=jax.ShapeDtypeStruct((tokens, chips * width), BF),
        interpret=INTERPRET,
        compiler_params=SMALL,
        name="combine",
    )(weight, in_vmem(rows))


def section_order(sections, blocks):
    count = sections * blocks * CAP
    order = np.zeros((sections, blocks, 2, CAP, 2 * count), np.float32)
    for p in range(sections):
        for y in range(blocks):
            for slot in range(CAP):
                for way, source in ((0, (p - 1) % sections), (1, (p + 1) % sections)):
                    order[p, y, way, slot, way * count + (source * blocks + y) * CAP + slot] = 1.0
    return order.reshape(2 * count, 2 * count)


def route_tables(routes, scores, groups):
    experts = jnp.arange(groups, dtype=jnp.int32)
    match = (routes[:, :, None] == experts).astype(F32)
    weight = 2.5 * scores / jnp.sum(scores, axis=-1, keepdims=True)
    hits = jnp.sum(match, axis=1)
    shares = jnp.sum(match * weight[:, :, None], axis=1)
    before = jnp.cumsum(hits, axis=0) - hits
    slots = jnp.arange(CAP, dtype=F32)
    placed = hits[:, :, None] * (before[:, :, None] == slots).astype(F32)
    return (placed, placed * shares[:, :, None])


def gather_rows(values, placed):
    return jnp.einsum(
        "tgc,td->gcd", placed.astype(BF), values, preferred_element_type=F32
    ).astype(BF)


def shifted(value, steps):
    count = lax.axis_size(PP)
    pairs = [(source, (source + steps) % count) for source in range(count)]
    return lax.ppermute(value, PP, pairs)


def all_to_all(value, axes):
    return lax.all_to_all(value, axes, split_axis=0, concat_axis=0, tiled=True)


def body(
    x_fwd, dy_bwd, routes_fwd, routes_bwd, score_fwd, score_bwd, saved_bwd, w_gate, w_up, w_down
):
    chips = lax.axis_size(CHIPS)
    sections = lax.axis_size(PP)
    ny = lax.axis_size("yhi")
    ns = lax.axis_size("z8")
    nz = lax.axis_size(Z)
    groups = 2 * ny
    width = w_gate.shape[0] // chips
    tokens = x_fwd.shape[1]
    core = lax.axis_index("core")

    packed = pack_weights(w_gate, w_up, w_down, width)
    weights = lax.all_gather(packed, Z, axis=0, tiled=True)
    weights = weights.reshape(nz, packed.shape[0], LANES)

    placed_f, weighted_f = route_tables(routes_fwd[0], score_fwd[0], groups)
    placed_b, weighted_b = route_tables(routes_bwd[0], score_bwd[0], groups)
    rows = jnp.stack([gather_rows(x_fwd[0], placed_f), gather_rows(dy_bwd[0], placed_b)])
    rows = rows.reshape(2, ny, 2, CAP, chips, width).transpose(4, 1, 0, 2, 3, 5)
    rows = jnp.broadcast_to(rows[:, None], (chips, 2) + rows.shape[1:])
    rows = all_to_all(rows.reshape(sections * ny, 4 * CAP, width), SPREAD)
    rows = rows.reshape(sections * ny, 2, 2, CAP, width).transpose(1, 2, 0, 3, 4)
    rows = rows.reshape(2, 2, sections * ny * CAP, width)

    saved = saved_bwd[0].astype(BF).reshape(ny, nz, CAP, 2, 2, HALF).transpose(4, 1, 0, 2, 3, 5)
    saved = all_to_all(saved.reshape(2 * nz, ny * CAP, LANES), ("core",) + Z)
    saved = saved.reshape(2, 2, ns, ny, CAP, 2, HALF).transpose(5, 1, 0, 3, 4, 2, 6)
    saved = saved.reshape(2, 2, 2 * ny * CAP, ns * HALF)

    mix_f = shifted(weighted_f.reshape(tokens, groups * CAP), 1)
    mix_b = shifted(weighted_b.reshape(tokens, groups * CAP), -1)
    mix = jnp.stack([mix_f, mix_b], axis=1).reshape(tokens, 2, ny, 2, CAP).transpose(0, 3, 2, 1, 4)
    mix = mix.reshape(tokens, 4 * ny * CAP)
    rows, saved, mix = lax.optimization_barrier((rows, saved, mix))

    parts = all_to_all(first_matmul(rows, weights, chips), CHIPS)
    hidden = all_to_all(activate(parts, saved[0], saved[1]), CHIPS)

    away = (1 - core).astype(jnp.int32).reshape(1)
    sent = second_matmul(away, hidden, weights, width, BF)
    other = lax.ppermute(sent, "core", [(0, 1), (1, 0)])
    kept = second_matmul(1 - away, hidden, weights, width, F32)
    order = jnp.asarray(section_order(sections, ny), BF)
    merged = merge(kept, other, order)
    merged = all_to_all(merged, SPREAD)
    return combine(mix, merged.reshape(chips, 4 * ny * CAP, width))[None]


def solution(mesh):
    fine = Mesh(mesh.devices.reshape(PARTS), NAMES)
    by_token = P(PP, EP, None)
    in_specs = (by_token,) * 6 + (
        P(PP, None, None, None, EP),
        P(None, EP),
        P(None, EP),
        P(EP, None),
    )
    return jax.shard_map(
        body, mesh=fine, in_specs=in_specs, out_specs=by_token, check_vma=False
    )
```

```python
import functools

import jax
import jax.numpy as jnp
import numpy as np
from jax import lax
from jax.experimental import pallas as pl
from jax.experimental.pallas import tpu as pltpu
from jax.sharding import Mesh, PartitionSpec as P

CAP = 2
LANES = 128
HALF = 64
PP = ("ylo", "x", "core")
EP = ("yhi", "zh", "z8")
CHIPS = ("ylo", "x")
Z = ("zh", "z8")
SPREAD = ("ylo", "x", "core", "yhi")
PARTS = (2, 4, 2, 4, 2, 8)
NAMES = PP + EP
INTERPRET = False
GROUP = 4
PAIR = 2
AHEAD = 2

BF = jnp.bfloat16
F32 = jnp.float32


def roll_half(value):
    return pltpu.roll(value, HALF, 1)


def low_lanes(shape):
    return lax.broadcasted_iota(jnp.int32, shape, len(shape) - 1) < HALF


def dot_nn(a, b):
    return lax.dot_general(a, b, (((1,), (0,)), ((), ())), preferred_element_type=F32)


def dot_nt(a, b):
    return lax.dot_general(a, b, (((1,), (1,)), ((), ())), preferred_element_type=F32)


def in_vmem(value):
    return value if INTERPRET else pltpu.with_memory_space_constraint(value, pltpu.VMEM)


def in_hbm(value):
    return value if INTERPRET else pltpu.with_memory_space_constraint(value, pltpu.HBM)


SMALL = pltpu.CompilerParams(vmem_limit_bytes=20 << 20)
VMEM_SPEC = pl.BlockSpec(memory_space=pltpu.VMEM)


def full(shape):
    return pl.BlockSpec(shape, lambda *_: (0,) * len(shape))


def pack_weights_kernel(gate, up, down, out, g_ref, u_ref, d_ref, sems):
    width = g_ref.shape[0]
    chip = lax.axis_index("ylo") * lax.axis_size("x") + lax.axis_index("x")
    core = lax.axis_index("core")
    rows = pl.ds(pl.multiple_of(chip * width, width), width)
    half = pl.ds(pl.multiple_of(core * HALF, HALF), HALF)
    copies = [
        pltpu.make_async_copy(gate.at[rows], g_ref, sems.at[0]),
        pltpu.make_async_copy(up.at[rows], u_ref, sems.at[1]),
        pltpu.make_async_copy(down.at[half, rows], d_ref, sems.at[2]),
    ]
    for copy in copies:
        copy.start()
    for copy in copies:
        copy.wait()
    first = core == 0
    g = g_ref[...].astype(F32)
    u = u_ref[...].astype(F32)
    low = low_lanes(g.shape)
    top = jnp.where(low, g, roll_half(u))
    bottom = jnp.where(low, roll_half(g), u)
    out[:width, :] = jnp.where(first, top, bottom).astype(BF)
    for i in range(width // LANES):
        out[width + HALF * i : width + HALF * (i + 1), :] = d_ref[:, LANES * i : LANES * (i + 1)]


def pack_weights(w_gate, w_up, w_down, width):
    rows = width + HALF * (width // LANES)
    return pl.pallas_call(
        pack_weights_kernel,
        in_specs=[pl.BlockSpec(memory_space=pl.ANY)] * 3,
        out_specs=VMEM_SPEC,
        out_shape=jax.ShapeDtypeStruct((rows, LANES), BF),
        scratch_shapes=[
            pltpu.VMEM((width, LANES), BF),
            pltpu.VMEM((width, LANES), BF),
            pltpu.VMEM((HALF, width), BF),
            pltpu.SemaphoreType.DMA((3,)),
        ],
        interpret=INTERPRET,
        compiler_params=SMALL,
        name="pack_weights",
    )(in_hbm(w_gate), in_hbm(w_up), in_hbm(w_down))


def down_rows(weights, at, count, width):
    tiles = []
    for i in range(width // LANES):
        lo = width + HALF * i
        parts = [weights[at + k, lo : lo + HALF] for k in range(count)]
        tiles.append(jnp.concatenate(parts, axis=0))
    return jnp.concatenate(tiles, axis=1)


def up_columns(weights, at, count, width):
    return jnp.concatenate([weights[at + k, :width] for k in range(count)], axis=1)


def first_matmul_kernel(rows, source, out, weights, sems):
    halves, count, width = rows.shape[1:]
    chips = out.shape[0]
    per_chip = count // chips
    total = weights.shape[0]
    copies = [
        pltpu.make_async_copy(
            source.at[GROUP * i : GROUP * (i + 1)], weights.at[GROUP * i : GROUP * (i + 1)], sems.at[i]
        )
        for i in range(total // GROUP)
    ]
    for copy in copies[:AHEAD]:
        copy.start()
    for i, copy in enumerate(copies):
        h, j = divmod(i, total // GROUP // halves)
        copy.wait()
        if i + AHEAD < len(copies):
            copies[i + AHEAD].start()
        pre = dot_nn(rows[0, h], up_columns(weights, GROUP * i, GROUP, width)).astype(BF)
        grad = dot_nt(rows[1, h], down_rows(weights, GROUP * i, GROUP, width)).astype(BF)
        for chip in range(chips):
            span = slice(chip * per_chip, (chip + 1) * per_chip)
            for k in range(GROUP // 2):
                at = 3 * LANES * (j * GROUP // 2 + k)
                out[chip, h, :, at : at + 2 * LANES] = pre[span, 2 * LANES * k : 2 * LANES * (k + 1)]
                out[chip, h, :, at + 2 * LANES : at + 3 * LANES] = grad[
                    span, LANES * k : LANES * (k + 1)
                ]


def first_matmul(rows, weights, chips):
    _, halves, count, _ = rows.shape
    total = weights.shape[0]
    shape = (chips, halves, count // chips, total // halves // 2 * 3 * LANES)
    return pl.pallas_call(
        first_matmul_kernel,
        in_specs=[VMEM_SPEC, pl.BlockSpec(memory_space=pl.ANY)],
        out_specs=VMEM_SPEC,
        out_shape=jax.ShapeDtypeStruct(shape, BF),
        scratch_shapes=[pltpu.VMEM(weights.shape, BF), pltpu.SemaphoreType.DMA((total // GROUP,))],
        interpret=INTERPRET,
        compiler_params=SMALL,
        name="first_matmul",
    )(in_vmem(rows), in_hbm(weights))


def activate_kernel(parts, gates, ups, out):
    chips = parts.shape[0]
    for h in range(parts.shape[1]):
        total = parts[0, h].astype(F32)
        for chip in range(1, chips):
            total = total + parts[chip, h].astype(F32)
        for j in range(parts.shape[3] // (3 * LANES)):
            at = 3 * LANES * j
            hidden = []
            for k in range(2):
                v = total[:, at + LANES * k : at + LANES * (k + 1)]
                hidden.append(v / (1.0 + jnp.exp(-v)) * roll_half(v))
            low = low_lanes(hidden[0].shape)
            hid = jnp.where(low, hidden[0], roll_half(hidden[1]))
            grad = total[:, at + 2 * LANES : at + 3 * LANES]
            gate = gates[h, :, LANES * j : LANES * (j + 1)].astype(F32)
            up = ups[h, :, LANES * j : LANES * (j + 1)].astype(F32)
            sigma = 1.0 / (1.0 + jnp.exp(-gate))
            grad_gate = grad * up * sigma * (1.0 + gate * (1.0 - sigma))
            grad_up = grad * gate * sigma
            tile = jnp.concatenate(
                [
                    jnp.where(low, grad_gate, roll_half(grad_up)),
                    jnp.where(low, roll_half(grad_gate), grad_up),
                    hid,
                ],
                axis=1,
            ).astype(BF)
            for chip in range(chips):
                out[chip, h, :, at : at + 3 * LANES] = tile


def activate(parts, gates, ups):
    return pl.pallas_call(
        activate_kernel,
        in_specs=[VMEM_SPEC] * 3,
        out_shape=jax.ShapeDtypeStruct(parts.shape, BF),
        interpret=INTERPRET,
        compiler_params=SMALL,
        name="activate",
    )(in_vmem(parts), in_vmem(gates), in_vmem(ups))


def second_matmul_kernel(half, hidden, source, out, weights, sems):
    h = half[0]
    width = out.shape[2]
    slices = weights.shape[0]
    copies = [
        pltpu.make_async_copy(
            source.at[pl.ds(slices * h + PAIR * j, PAIR)],
            weights.at[PAIR * j : PAIR * (j + 1)],
            sems.at[j],
        )
        for j in range(slices // PAIR)
    ]
    for copy in copies[:AHEAD]:
        copy.start()
    rows = jnp.concatenate([hidden[chip, h] for chip in range(hidden.shape[0])], axis=0)
    fwd = None
    bwd = None
    for j, copy in enumerate(copies):
        copy.wait()
        if j + AHEAD < len(copies):
            copies[j + AHEAD].start()
        ats = [3 * LANES * (j * PAIR // 2 + k) for k in range(PAIR // 2)]
        hid = jnp.concatenate([rows[:, at + 2 * LANES : at + 3 * LANES] for at in ats], axis=1)
        grads = jnp.concatenate([rows[:, at : at + 2 * LANES] for at in ats], axis=1)
        more_f = dot_nn(hid, down_rows(weights, PAIR * j, PAIR, width))
        more_b = dot_nt(grads, up_columns(weights, PAIR * j, PAIR, width))
        fwd = more_f if fwd is None else fwd + more_f
        bwd = more_b if bwd is None else bwd + more_b
    out[0] = fwd.astype(out.dtype)
    out[1] = bwd.astype(out.dtype)


def second_matmul(half, hidden, weights, width, dtype):
    chips, halves, per_chip, _ = hidden.shape
    slices = weights.shape[0] // halves
    return pl.pallas_call(
        second_matmul_kernel,
        in_specs=[
            pl.BlockSpec(memory_space=pltpu.SMEM),
            VMEM_SPEC,
            pl.BlockSpec(memory_space=pl.ANY),
        ],
        out_specs=VMEM_SPEC,
        out_shape=jax.ShapeDtypeStruct((2, chips * per_chip, width), dtype),
        scratch_shapes=[
            pltpu.VMEM((slices,) + weights.shape[1:], BF),
            pltpu.SemaphoreType.DMA((slices // PAIR,)),
        ],
        interpret=INTERPRET,
        compiler_params=SMALL,
        name="second_matmul",
    )(half, in_vmem(hidden), in_hbm(weights))


def merge_kernel(kept, other, order, out):
    count = kept.shape[1]
    total = (kept[...] + other[...].astype(F32)).astype(BF)
    moved = dot_nn(order[...], total.reshape(2 * count, total.shape[2]))
    rows = out.shape[1]
    for i in range(out.shape[0]):
        out[i] = moved[rows * i : rows * (i + 1)].astype(BF)


def merge(kept, other, order):
    _, count, width = kept.shape
    return pl.pallas_call(
        merge_kernel,
        in_specs=[VMEM_SPEC] * 3,
        out_shape=jax.ShapeDtypeStruct((count // CAP, 2 * CAP, width), BF),
        interpret=INTERPRET,
        compiler_params=SMALL,
        name="merge",
    )(in_vmem(kept), in_vmem(other), in_vmem(order))


def combine_kernel(weight, rows, out):
    w = weight[...]
    top = w.astype(BF)
    rest = w - top.astype(F32)
    mid = rest.astype(BF)
    low = (rest - mid.astype(F32)).astype(BF)
    stacked = jnp.concatenate([top, mid, low], axis=0)
    tokens = w.shape[0]
    width = rows.shape[2]
    for chip in range(rows.shape[0]):
        parts = dot_nn(stacked, rows[chip])
        total = parts[:tokens] + (parts[tokens : 2 * tokens] + parts[2 * tokens :])
        out[:, width * chip : width * (chip + 1)] = total.astype(BF)


def combine(weight, rows):
    chips, depth, width = rows.shape
    tokens = weight.shape[0]
    step = max(1, chips // 2)
    return pl.pallas_call(
        combine_kernel,
        grid=(chips // step,),
        in_specs=[full(weight.shape), pl.BlockSpec((step, depth, width), lambda q: (q, 0, 0))],
        out_specs=pl.BlockSpec((tokens, step * width), lambda q: (0, q)),
        out_shape=jax.ShapeDtypeStruct((tokens, chips * width), BF),
        interpret=INTERPRET,
        compiler_params=SMALL,
        name="combine",
    )(weight, in_vmem(rows))


def section_order(sections, blocks):
    count = sections * blocks * CAP
    order = np.zeros((sections, blocks, 2, CAP, 2 * count), np.float32)
    for p in range(sections):
        for y in range(blocks):
            for slot in range(CAP):
                for way, source in ((0, (p - 1) % sections), (1, (p + 1) % sections)):
                    order[p, y, way, slot, way * count + (source * blocks + y) * CAP + slot] = 1.0
    return order.reshape(2 * count, 2 * count)


def route_tables(routes, scores, groups):
    experts = jnp.arange(groups, dtype=jnp.int32)
    match = (routes[:, :, None] == experts).astype(F32)
    weight = 2.5 * scores / jnp.sum(scores, axis=-1, keepdims=True)
    hits = jnp.sum(match, axis=1)
    shares = jnp.sum(match * weight[:, :, None], axis=1)
    before = jnp.cumsum(hits, axis=0) - hits
    slots = jnp.arange(CAP, dtype=F32)
    placed = hits[:, :, None] * (before[:, :, None] == slots).astype(F32)
    return (placed, placed * shares[:, :, None])


def gather_rows(values, placed):
    return jnp.einsum(
        "tgc,td->gcd", placed.astype(BF), values, preferred_element_type=F32
    ).astype(BF)


def shifted(value, steps):
    count = lax.axis_size(PP)
    pairs = [(source, (source + steps) % count) for source in range(count)]
    return lax.ppermute(value, PP, pairs)


def all_to_all(value, axes):
    return lax.all_to_all(value, axes, split_axis=0, concat_axis=0, tiled=True)


def body(
    x_fwd, dy_bwd, routes_fwd, routes_bwd, score_fwd, score_bwd, saved_bwd, w_gate, w_up, w_down
):
    chips = lax.axis_size(CHIPS)
    sections = lax.axis_size(PP)
    ny = lax.axis_size("yhi")
    ns = lax.axis_size("z8")
    nz = lax.axis_size(Z)
    groups = 2 * ny
    width = w_gate.shape[0] // chips
    tokens = x_fwd.shape[1]
    core = lax.axis_index("core")

    packed = pack_weights(w_gate, w_up, w_down, width)
    weights = lax.all_gather(packed, Z, axis=0, tiled=True)
    weights = weights.reshape(nz, packed.shape[0], LANES)

    placed_f, weighted_f = route_tables(routes_fwd[0], score_fwd[0], groups)
    placed_b, weighted_b = route_tables(routes_bwd[0], score_bwd[0], groups)
    rows = jnp.stack([gather_rows(x_fwd[0], placed_f), gather_rows(dy_bwd[0], placed_b)])
    rows = rows.reshape(2, ny, 2, CAP, chips, width).transpose(4, 1, 0, 2, 3, 5)
    rows = jnp.broadcast_to(rows[:, None], (chips, 2) + rows.shape[1:])
    rows = all_to_all(rows.reshape(sections * ny, 4 * CAP, width), SPREAD)
    rows = rows.reshape(sections * ny, 2, 2, CAP, width).transpose(1, 2, 0, 3, 4)
    rows = rows.reshape(2, 2, sections * ny * CAP, width)

    saved = saved_bwd[0].astype(BF).reshape(ny, nz, CAP, 2, 2, HALF).transpose(4, 1, 0, 2, 3, 5)
    saved = all_to_all(saved.reshape(2 * nz, ny * CAP, LANES), ("core",) + Z)
    saved = saved.reshape(2, 2, ns, ny, CAP, 2, HALF).transpose(5, 1, 0, 3, 4, 2, 6)
    saved = saved.reshape(2, 2, 2 * ny * CAP, ns * HALF)

    mix_f = shifted(weighted_f.reshape(tokens, groups * CAP), 1)
    mix_b = shifted(weighted_b.reshape(tokens, groups * CAP), -1)
    mix = jnp.stack([mix_f, mix_b], axis=1).reshape(tokens, 2, ny, 2, CAP).transpose(0, 3, 2, 1, 4)
    mix = mix.reshape(tokens, 4 * ny * CAP)
    rows, saved, mix = lax.optimization_barrier((rows, saved, mix))

    parts = all_to_all(first_matmul(rows, weights, chips), CHIPS)
    hidden = all_to_all(activate(parts, saved[0], saved[1]), CHIPS)

    away = (1 - core).astype(jnp.int32).reshape(1)
    sent = second_matmul(away, hidden, weights, width, BF)
    other = lax.ppermute(sent, "core", [(0, 1), (1, 0)])
    kept = second_matmul(1 - away, hidden, weights, width, F32)
    order = jnp.asarray(section_order(sections, ny), BF)
    merged = merge(kept, other, order)
    merged = all_to_all(merged, SPREAD)
    return combine(mix, merged.reshape(chips, 4 * ny * CAP, width))[None]


def solution(mesh):
    fine = Mesh(mesh.devices.reshape(PARTS), NAMES)
    by_token = P(PP, EP, None)
    in_specs = (by_token,) * 6 + (
        P(PP, None, None, None, EP),
        P(None, EP),
        P(None, EP),
        P(EP, None),
    )
    return jax.shard_map(
        body, mesh=fine, in_specs=in_specs, out_specs=by_token, check_vma=False
    )
```
